256 devices in a mesh: prow: 32 (over y, z), pcol: 8 (over x, core).
Axes of the slice: x: 4, y: 4, z: 8, core: 2. Of those that a mesh axis runs over, the one named last changes fastest.
Arguments:
- panel_rows: float32 [2, 1024, 98304], P(None, None, ('prow', 'pcol')), may hold values from -0.078125 to 0.078125
- solved: float32 [98304, 1024], P(('prow', 'pcol')), may hold values from -6 to 6
- right_side: float32 [2, 1024, 1024], P(None, 'prow', 'pcol'), may hold values from -6 to 6
- coupling: float32 [1024, 1024], P(None, 'prow'), may hold values from -0.1875 to 0.1875
- inverses: float32 [2, 1024, 1024], P(None, 'prow'), may hold values from -2 to 2, as said below
Outputs:
- panels: float32 [2, 1024, 1024], P(None, 'prow', 'pcol')
The draws below stay inside these ranges and needn't reach their ends.
Inputs may be any that keep to these rules, and one draw needn't show every extreme that they name: `inverses`: each tile is zero above its diagonal, and its diagonal entries are positive.
All inputs are finite; a program needn't handle non-finite values.
Results may differ from the reference program's by a relative error of at most 0.000088.
Values sent between devices are 32-bit elements; how exact they have to be, the bound alone decides.
No kernel may reach another device: no remote copies, remote signals or barrier semaphores. Data moves between devices by JAX's collectives and lax.ppermute only.
A program may use at most 64 MiB of HBM per device.

```python
import jax
import jax.numpy as jnp
from jax import lax

NB = 1024
RHS = 1024
SOLVED = 98304


def draw_inverses(key, part):
    keyed = jax.random.fold_in(key, 31)
    key_lower, key_diag = jax.random.split(keyed)
    reach = jnp.sqrt(3.0 / NB)
    lower_part = jax.random.uniform(key_lower, (2, NB, NB), jnp.float32, -reach, reach)
    diag_values = jax.random.uniform(key_diag, (2, NB), jnp.float32, 0.5, 1.5)
    lower_part = jnp.tril(lower_part, -1)
    identity = jnp.eye(NB, dtype=jnp.float32)
    return lower_part + diag_values[:, :, None] * identity[None, :, :]


def spiked(values, rng, source, target, shards_of, factor):
    owner, partner = [(jnp.arange(values.shape[dim]) // (values.shape[dim] // shards_of)).reshape([-1 if axis == dim else 1 for axis in range(values.ndim)]) for dim in (source, target)]
    chosen = jax.random.permutation(rng, shards_of)[partner]
    strong = (owner == chosen) | (owner == (partner + shards_of // 2) % shards_of)
    return jnp.where(strong, factor * values, values)


def block_levels(rng, extent, cuts, least, high):
    gain = 1.0
    for dim, blocks in cuts:
        draws = jax.random.uniform(jax.random.fold_in(jax.random.fold_in(rng, 6), dim), (blocks,), jnp.float32, least / len(cuts), high / len(cuts))
        gain = gain * jnp.repeat(jnp.exp(draws), extent[dim] // blocks).reshape((-1,) + (1,) * (len(extent) - 1 - dim))
    return gain


def gaussian(own_key, extent, spread, most, cuts=(), kind=jnp.bfloat16):
    entries = spread * jax.random.normal(own_key, extent, jnp.float32)
    if cuts:
        entries = entries * block_levels(own_key, extent, cuts, -0.22, 0.18)
    return jnp.clip(entries, -most, most).astype(kind)


def noise_with(key, shape, scale, bound, shards, heavy, held_as=jnp.bfloat16):
    entries = scale * jax.random.normal(key, shape, jnp.float32)
    if shards:
        entries = entries * block_levels(key, shape, shards, -0.22, 0.18)
    return jnp.clip(spiked(entries, jax.random.fold_in(key, 3), *heavy), -bound, bound).astype(held_as)


def setup_inputs(seed: int = 0) -> dict:
    seeds = jax.random.split(jax.random.key(seed), 6)
    return {
        "panel_rows": noise_with(seeds[0], (2, NB, SOLVED), SOLVED ** -0.5, 0.078125, ((2, 256),), (2, 1, 256, 6.0), jnp.float32),
        "solved": gaussian(seeds[1], (SOLVED, RHS), 1.0, 6.0, ((0, 256),), jnp.float32),
        "right_side": gaussian(seeds[2], (2, NB, RHS), 1.0, 6.0, ((1, 32), (2, 8)), jnp.float32),
        "coupling": gaussian(seeds[3], (NB, NB), NB ** -0.5, 0.1875, ((1, 32),), jnp.float32),
        "inverses": draw_inverses(jax.random.fold_in(seeds[5], 71), 0),
    }


def reference(panel_rows, solved, right_side, coupling, inverses):
    highest = lax.Precision.HIGHEST
    old_first = jnp.dot(panel_rows[0], solved, precision=highest, preferred_element_type=jnp.float32)
    old_second = jnp.dot(panel_rows[1], solved, precision=highest, preferred_element_type=jnp.float32)
    first_rest = right_side[0] - old_first
    first_panel = jnp.dot(inverses[0], first_rest, precision=highest, preferred_element_type=jnp.float32)
    coupled = jnp.dot(coupling, first_panel, precision=highest, preferred_element_type=jnp.float32)
    second_rest = right_side[1] - old_second - coupled
    second_panel = jnp.dot(inverses[1], second_rest, precision=highest, preferred_element_type=jnp.float32)
    return jnp.stack([first_panel, second_panel])
```

```python
import jax
import jax.numpy as jnp
from jax import lax
from jax.experimental import pallas as pl
from jax.experimental.pallas import tpu as pltpu
from jax.sharding import Mesh
from jax.sharding import PartitionSpec as P


AXES = ("y", "z", "x", "core")
F32 = jnp.float32
BF16 = jnp.bfloat16
EXACT = lax.Precision.HIGHEST
SMEM = pl.BlockSpec(memory_space=pltpu.SMEM)
SMALL = pltpu.CompilerParams(vmem_limit_bytes=4 << 20)


def shift(value, axis, step, size):
    return lax.ppermute(value, axis, [(i, (i + step) % size) for i in range(size)])


def halves(value):
    high = value.astype(BF16)
    return high, (value - high.astype(F32)).astype(BF16)


def product_kernel(by_column, has_received, nx, ny):
    def kernel(place, rows, cols, *refs):
        received = refs[0] if has_received else None
        outs = refs[1:-2] if has_received else refs[:-2]
        left, right = refs[-2:]
        depth = rows.shape[1]
        high_rows = rows.shape[0] // ny
        for jx in range(nx):
            at = lax.rem(place[0] + jx, nx) * 256 + place[2] * 128
            high, low = halves(cols[:, pl.ds(pl.multiple_of(at, 128), 128)])
            span = slice(jx * 128, (jx + 1) * 128)
            right[0:depth, span] = high
            right[depth : 2 * depth, span] = low
            right[2 * depth : 3 * depth, span] = high
        for jy in range(ny):
            at = lax.rem(place[1] + jy, ny) * high_rows
            high, low = halves(rows[pl.ds(pl.multiple_of(at, high_rows), high_rows), :])
            left[:, 0:depth] = high
            left[:, depth : 2 * depth] = high
            left[:, 2 * depth : 3 * depth] = low
            value = jnp.dot(left[...], right[...], preferred_element_type=F32)
            for jx in range(nx):
                block = value[:, jx * 128 : (jx + 1) * 128]
                first, second = (jx, jy) if by_column else (jy, jx)
                span = slice(second * high_rows, (second + 1) * high_rows)
                if has_received:
                    outs[first][span, :] = block + received[first, span, :]
                else:
                    outs[0][first, span, :] = block

    return kernel


def products(place, rows, cols, received, by_column, nx, ny):
    kernel = product_kernel(by_column, received is not None, nx, ny)
    depth = rows.shape[1]
    size = rows.shape[0]
    first = nx if by_column else ny
    if received is None:
        shapes = jax.ShapeDtypeStruct((first, size, 128), F32)
        args = (place, rows, cols)
    else:
        shapes = [jax.ShapeDtypeStruct((size, 128), F32)] * first
        args = (place, rows, cols, received)
    return pl.pallas_call(
        kernel,
        out_shape=shapes,
        in_specs=[SMEM] + [pl.BlockSpec()] * (len(args) - 1),
        scratch_shapes=[
            pltpu.VMEM((size // ny, 3 * depth), BF16),
            pltpu.VMEM((3 * depth, nx * 128), BF16),
        ],
        compiler_params=pltpu.CompilerParams(vmem_limit_bytes=16 << 20),
        cost_estimate=pl.CostEstimate(
            flops=6 * size * depth * nx * 128, transcendentals=0, bytes_accessed=6 << 20
        ),
    )(*args)


def pack_kernel(place, inverses, across, out):
    at = pl.multiple_of(place[0] * 256 + place[2] * 128, 128)
    strip_of_coupling = across[:, pl.ds(at, 128)]
    strip_of_second = inverses[1, :, pl.ds(at, 128)]
    nz = out.shape[0]
    for z in range(nz):
        out[z, :, 0:128] = strip_of_coupling
        out[z, :, 128:256] = strip_of_second
        for panel in range(2):
            pieces = [inverses[panel, :, y * 256 + z * 32 : y * 256 + z * 32 + 32] for y in range(4)]
            out[z, :, 256 + panel * 128 : 384 + panel * 128] = jnp.concatenate(pieces, axis=1)


def couple_kernel(tiles, out):
    out[...] = lax.dot_general(
        tiles[:, 0:128],
        tiles[:, 256:384],
        (((0,), (0,)), ((), ())),
        precision=EXACT,
        preferred_element_type=F32,
    )


def chain_kernel(tiles, part0, part1, part2, part3, out):
    total = (part0[...] + part1[...]) + (part2[...] + part3[...])
    out[...] = jnp.dot(tiles[:, 128:256], total, precision=EXACT, preferred_element_type=F32)


def apply_kernel(place, tiles, mix0, mix1, mix2, mix3, rest0, rest1, rest2, rest3, out, first, second):
    ny = 4
    for step, rest in enumerate((rest0, rest1, rest2, rest3)):
        at = pl.multiple_of(lax.rem(place[1] + ny - step, ny) * 32, 32)
        first[pl.ds(at, 32), :] = rest[0:32, :]
        second[pl.ds(at, 32), :] = rest[32:64, :]
    mix = (mix0[...] + mix1[...]) + (mix2[...] + mix3[...])
    low = jnp.dot(tiles[:, 256:384], first[...], precision=EXACT, preferred_element_type=F32)
    high = jnp.dot(tiles[:, 384:512], second[...], precision=EXACT, preferred_element_type=F32)
    high = high - jnp.dot(mix, first[...], precision=EXACT, preferred_element_type=F32)
    for z in range(out.shape[0]):
        out[z, 0:32, :] = low[z * 32 : (z + 1) * 32, :]
        out[z, 32:64, :] = high[z * 32 : (z + 1) * 32, :]


def interleave_kernel(a0, a1, a2, a3, b0, b1, b2, b3, out):
    low = (a0[...] + a1[...]) + (a2[...] + a3[...])
    high = (b0[...] + b1[...]) + (b2[...] + b3[...])
    for z in range(out.shape[0]):
        out[z, 0:32, :] = low[z * 32 : (z + 1) * 32, :]
        out[z, 32:64, :] = high[z * 32 : (z + 1) * 32, :]


def summed_blocks(parts, count):
    rows = parts[0].shape[0] // count
    out = []
    for j in range(count):
        a, b, c, d = [part[j * rows : (j + 1) * rows] for part in parts]
        out.append((a + b) + (c + d))
    return out


def body(panel_rows, solved, right_side, coupling, inverses):
    nx, ny, nz, nc = (lax.axis_size(a) for a in ("x", "y", "z", "core"))
    x, y, core = lax.axis_index("x"), lax.axis_index("y"), lax.axis_index("core")
    own = jnp.stack([x, y, core]).astype(jnp.int32)
    other = jnp.stack([x, y, 1 - core]).astype(jnp.int32)

    to_partner0 = products(other, panel_rows[0], solved, None, True, nx, ny)
    from_partner0 = shift(to_partner0, "core", 1, nc)
    to_partner1 = products(other, panel_rows[1], solved, None, False, nx, ny)
    from_partner1 = shift(to_partner1, "core", 1, nc)
    blocks0 = products(own, panel_rows[0], solved, from_partner0, True, nx, ny)
    got0 = [blocks0[0]] + [shift(blocks0[j], "x", j, nx) for j in range(1, nx)]
    blocks1 = products(own, panel_rows[1], solved, from_partner1, False, nx, ny)
    got1 = [blocks1[0]] + [shift(blocks1[j], "y", j, ny) for j in range(1, ny)]

    packed = pl.pallas_call(
        pack_kernel,
        out_shape=jax.ShapeDtypeStruct((nz, 32, 512), F32),
        in_specs=[SMEM, pl.BlockSpec(), pl.BlockSpec()],
        compiler_params=SMALL,
    )(own, inverses, coupling.T)
    tiles = lax.all_to_all(packed, "z", 0, 0, tiled=True).reshape(nz * 32, 512)
    coupled = pl.pallas_call(
        couple_kernel, out_shape=jax.ShapeDtypeStruct((128, 128), F32), compiler_params=SMALL
    )(tiles)
    coupled_all = [coupled] + [shift(coupled, "y", j, ny) for j in range(1, ny)]
    chained = pl.pallas_call(
        chain_kernel, out_shape=jax.ShapeDtypeStruct((256, 128), F32), compiler_params=SMALL
    )(
        tiles, *coupled_all
    )
    chained = chained + shift(chained, "core", 1, nc)
    mixes = [chained] + [shift(chained, "x", j, nx) for j in range(1, nx)]

    sums0 = summed_blocks(got0, ny)
    again0 = [sums0[0]] + [shift(sums0[j], "y", j, ny) for j in range(1, ny)]
    sums1 = summed_blocks(got1, nx)
    again1 = [sums1[0]] + [shift(sums1[j], "x", j, nx) for j in range(1, nx)]
    by_z = pl.pallas_call(
        interleave_kernel, out_shape=jax.ShapeDtypeStruct((nz, 64, 128), F32), compiler_params=SMALL
    )(
        *again0, *again1
    )
    old = lax.all_to_all(by_z, "z", 0, 0, tiled=True).sum(axis=0)
    rest = right_side.reshape(64, 128) - old

    rests = [rest] + [shift(rest, "y", j, ny) for j in range(1, ny)]
    solved_part = pl.pallas_call(
        apply_kernel,
        out_shape=jax.ShapeDtypeStruct((nz, 64, 128), F32),
        in_specs=[SMEM] + [pl.BlockSpec()] * 9,
        scratch_shapes=[pltpu.VMEM((128, 128), F32), pltpu.VMEM((128, 128), F32)],
        compiler_params=SMALL,
    )(own, tiles, *mixes, *rests)
    panels = lax.all_to_all(solved_part, "z", 0, 0, tiled=True).sum(axis=0)
    return panels.reshape(right_side.shape)


def solution(mesh):
    finer = Mesh(mesh.devices.reshape(4, 8, 4, 2), AXES)
    prow, pcol = ("y", "z"), ("x", "core")
    return jax.shard_map(
        body,
        mesh=finer,
        in_specs=(
            P(None, None, AXES),
            P(AXES, None),
            P(None, prow, pcol),
            P(None, prow),
            P(None, prow, None),
        ),
        out_specs=P(None, prow, pcol),
        check_vma=False,
    )
```

```python
import jax
import jax.numpy as jnp
from jax import lax
from jax.experimental import pallas as pl
from jax.experimental.pallas import tpu as pltpu
from jax.sharding import Mesh
from jax.sharding import PartitionSpec as P


AXES = ("y", "z", "x", "core")
F32 = jnp.float32
BF16 = jnp.bfloat16
EXACT = lax.Precision.HIGHEST
SMEM = pl.BlockSpec(memory_space=pltpu.SMEM)
ORDER = pl.BlockSpec(memory_space=pl.ANY)
SMALL = pltpu.CompilerParams(vmem_limit_bytes=4 << 20)


def shift(value, axis, step, size):
    return lax.ppermute(value, axis, [(i, (i + step) % size) for i in range(size)])


def halves(value):
    high = value.astype(BF16)
    return high, (value - high.astype(F32)).astype(BF16)


def product_kernel(by_column, has_received, nx, ny):
    def kernel(place, rows, cols, *refs):
        received = refs[0] if has_received else None
        outs = refs[1:-2] if has_received else refs[:-2]
        left, right = refs[-2:]
        depth = rows.shape[1]
        high_rows = rows.shape[0] // ny
        for jx in range(nx):
            at = lax.rem(place[0] + jx, nx) * 256 + place[2] * 128
            high, low = halves(cols[:, pl.ds(pl.multiple_of(at, 128), 128)])
            span = slice(jx * 128, (jx + 1) * 128)
            right[0:depth, span] = high
            right[depth : 2 * depth, span] = low
            right[2 * depth : 3 * depth, span] = high
        for jy in range(ny):
            at = lax.rem(place[1] + jy, ny) * high_rows
            high, low = halves(rows[pl.ds(pl.multiple_of(at, high_rows), high_rows), :])
            left[:, 0:depth] = high
            left[:, depth : 2 * depth] = high
            left[:, 2 * depth : 3 * depth] = low
            value = jnp.dot(left[...], right[...], preferred_element_type=F32)
            for jx in range(nx):
                block = value[:, jx * 128 : (jx + 1) * 128]
                first, second = (jx, jy) if by_column else (jy, jx)
                span = slice(second * high_rows, (second + 1) * high_rows)
                if has_received:
                    outs[first][span, :] = block + received[first, span, :]
                else:
                    outs[0][first, span, :] = block

    return kernel


def products(place, panel, rows, cols, received, by_column, nx, ny):
    kernel = product_kernel(by_column, received is not None, nx, ny)
    _, size, depth = rows.shape
    first = nx if by_column else ny
    if received is None:
        shapes = jax.ShapeDtypeStruct((first, size, 128), F32)
        args = (place, rows, cols)
    else:
        shapes = [jax.ShapeDtypeStruct((size, 128), F32)] * first
        args = (place, rows, cols, received)
    return pl.pallas_call(
        kernel,
        out_shape=shapes,
        grid=(1,),
        in_specs=[
            SMEM,
            pl.BlockSpec((pl.Squeezed(), size, depth), lambda i: (panel, 0, 0)),
        ]
        + [pl.BlockSpec()] * (len(args) - 2),
        scratch_shapes=[
            pltpu.VMEM((size // ny, 3 * depth), BF16),
            pltpu.VMEM((3 * depth, nx * 128), BF16),
        ],
        compiler_params=pltpu.CompilerParams(vmem_limit_bytes=16 << 20),
        cost_estimate=pl.CostEstimate(
            flops=6 * size * depth * nx * 128, transcendentals=0, bytes_accessed=6 << 20
        ),
    )(*args)


def pack_kernel(place, inverses, across, out):
    at = pl.multiple_of(place[0] * 256 + place[2] * 128, 128)
    strip_of_coupling = across[:, pl.ds(at, 128)]
    strip_of_second = inverses[1, :, pl.ds(at, 128)]
    nz = out.shape[0]
    for z in range(nz):
        out[z, :, 0:128] = strip_of_coupling
        out[z, :, 128:256] = strip_of_second
        for panel in range(2):
            pieces = [inverses[panel, :, y * 256 + z * 32 : y * 256 + z * 32 + 32] for y in range(4)]
            out[z, :, 256 + panel * 128 : 384 + panel * 128] = jnp.concatenate(pieces, axis=1)


def couple_kernel(tiles, out):
    out[...] = lax.dot_general(
        tiles[:, 0:128],
        tiles[:, 256:384],
        (((0,), (0,)), ((), ())),
        precision=EXACT,
        preferred_element_type=F32,
    )


def chain_kernel(tiles, part0, part1, part2, part3, out):
    total = (part0[...] + part1[...]) + (part2[...] + part3[...])
    out[...] = jnp.dot(tiles[:, 128:256], total, precision=EXACT, preferred_element_type=F32)


def apply_kernel(place, tiles, mix0, mix1, mix2, mix3, rest0, rest1, rest2, rest3, out, first, second):
    ny = 4
    for step, rest in enumerate((rest0, rest1, rest2, rest3)):
        at = pl.multiple_of(lax.rem(place[1] + ny - step, ny) * 32, 32)
        first[pl.ds(at, 32), :] = rest[0:32, :]
        second[pl.ds(at, 32), :] = rest[32:64, :]
    mix = (mix0[...] + mix1[...]) + (mix2[...] + mix3[...])
    low = jnp.dot(tiles[:, 256:384], first[...], precision=EXACT, preferred_element_type=F32)
    high = jnp.dot(tiles[:, 384:512], second[...], precision=EXACT, preferred_element_type=F32)
    high = high - jnp.dot(mix, first[...], precision=EXACT, preferred_element_type=F32)
    for z in range(out.shape[0]):
        out[z, 0:32, :] = low[z * 32 : (z + 1) * 32, :]
        out[z, 32:64, :] = high[z * 32 : (z + 1) * 32, :]


def interleave_kernel(a0, a1, a2, a3, b0, b1, b2, b3, after, out):
    low = (a0[...] + a1[...]) + (a2[...] + a3[...])
    high = (b0[...] + b1[...]) + (b2[...] + b3[...])
    for z in range(out.shape[0]):
        out[z, 0:32, :] = low[z * 32 : (z + 1) * 32, :]
        out[z, 32:64, :] = high[z * 32 : (z + 1) * 32, :]


def summed_blocks(parts, count):
    rows = parts[0].shape[0] // count
    out = []
    for j in range(count):
        a, b, c, d = [part[j * rows : (j + 1) * rows] for part in parts]
        out.append((a + b) + (c + d))
    return out


def steps(panel_rows, solved, right_side, coupling, inverses):
    nx, ny, nz, nc = (lax.axis_size(a) for a in ("x", "y", "z", "core"))
    x, y, core = lax.axis_index("x"), lax.axis_index("y"), lax.axis_index("core")
    own = jnp.stack([x, y, core]).astype(jnp.int32)
    other = jnp.stack([x, y, 1 - core]).astype(jnp.int32)

    to_partner0 = products(other, 0, panel_rows, solved, None, True, nx, ny)
    from_partner0 = shift(to_partner0, "core", 1, nc)
    to_partner1 = products(other, 1, panel_rows, solved, None, False, nx, ny)
    from_partner1 = shift(to_partner1, "core", 1, nc)
    blocks0 = products(own, 0, panel_rows, solved, from_partner0, True, nx, ny)
    got0 = [blocks0[0]] + [shift(blocks0[j], "x", j, nx) for j in range(1, nx)]
    blocks1 = products(own, 1, panel_rows, solved, from_partner1, False, nx, ny)
    got1 = [blocks1[0]] + [shift(blocks1[j], "y", j, ny) for j in range(1, ny)]

    packed = pl.pallas_call(
        pack_kernel,
        out_shape=jax.ShapeDtypeStruct((nz, 32, 512), F32),
        in_specs=[SMEM, pl.BlockSpec(), pl.BlockSpec()],
        compiler_params=SMALL,
    )(own, inverses, coupling.T)
    tiles = lax.all_to_all(packed, "z", 0, 0, tiled=True).reshape(nz * 32, 512)
    coupled = pl.pallas_call(
        couple_kernel, out_shape=jax.ShapeDtypeStruct((128, 128), F32), compiler_params=SMALL
    )(tiles)
    coupled_all = [coupled] + [shift(coupled, "y", j, ny) for j in range(1, ny)]
    chained = pl.pallas_call(
        chain_kernel, out_shape=jax.ShapeDtypeStruct((256, 128), F32), compiler_params=SMALL
    )(
        tiles, *coupled_all
    )
    both = chained + shift(chained, "core", 1, nc)
    mixes = [both] + [shift(both, "x", j, nx) for j in range(1, nx)]

    sums0 = summed_blocks(got0, ny)
    again0 = [sums0[0]] + [shift(sums0[j], "y", j, ny) for j in range(1, ny)]
    sums1 = summed_blocks(got1, nx)
    again1 = [sums1[0]] + [shift(sums1[j], "x", j, nx) for j in range(1, nx)]
    by_z = pl.pallas_call(
        interleave_kernel,
        out_shape=jax.ShapeDtypeStruct((nz, 64, 128), F32),
        in_specs=[pl.BlockSpec()] * 8 + [ORDER],
        compiler_params=SMALL,
    )(*again0, *again1, chained)
    old = lax.all_to_all(by_z, "z", 0, 0, tiled=True).sum(axis=0)
    rest = right_side.reshape(64, 128) - old

    rests = [rest] + [shift(rest, "y", j, ny) for j in range(1, ny)]
    solved_part = pl.pallas_call(
        apply_kernel,
        out_shape=jax.ShapeDtypeStruct((nz, 64, 128), F32),
        in_specs=[SMEM] + [pl.BlockSpec()] * 9,
        scratch_shapes=[pltpu.VMEM((128, 128), F32), pltpu.VMEM((128, 128), F32)],
        compiler_params=SMALL,
    )(own, tiles, *mixes, *rests)
    panels = lax.all_to_all(solved_part, "z", 0, 0, tiled=True).sum(axis=0)
    return panels.reshape(right_side.shape)


def solution(mesh):
    finer = Mesh(mesh.devices.reshape(4, 8, 4, 2), AXES)
    prow, pcol = ("y", "z"), ("x", "core")
    return jax.shard_map(
        steps,
        mesh=finer,
        in_specs=(
            P(None, None, AXES),
            P(AXES, None),
            P(None, prow, pcol),
            P(None, prow),
            P(None, prow, None),
        ),
        out_specs=P(None, prow, pcol),
        check_vma=False,
    )
```

```python
import jax
import jax.numpy as jnp
from jax import lax
from jax.experimental import pallas as pl
from jax.experimental.pallas import tpu as pltpu
from jax.sharding import Mesh
from jax.sharding import PartitionSpec as P


AXES = ("y", "z", "x", "core")
F32 = jnp.float32
BF16 = jnp.bfloat16
EXACT = lax.Precision.HIGHEST
SMEM = pl.BlockSpec(memory_space=pltpu.SMEM)
FAR = pl.BlockSpec(memory_space=pltpu.HBM)
SMALL = pltpu.CompilerParams(vmem_limit_bytes=6 << 20)


def shift(value, axis, step, size):
    return lax.ppermute(value, axis, [(i, (i + step) % size) for i in range(size)])


def halves(value):
    high = value.astype(BF16)
    return high, (value - high.astype(F32)).astype(BF16)


def product_kernel(panel, by_column, has_received, nx, ny):
    def kernel(place, rows, cols, *refs):
        received = refs[0] if has_received else None
        outs = refs[1:-5] if has_received else refs[:-5]
        left, right, strips, blocks, sems = refs[-5:]
        depth = cols.shape[0]
        size = blocks.shape[1]
        copies = []
        for jx in range(nx):
            at = pl.multiple_of(lax.rem(place[0] + jx, nx) * 256 + place[2] * 128, 128)
            copies.append(
                pltpu.make_async_copy(cols.at[:, pl.ds(at, 128)], strips.at[jx], sems.at[jx])
            )
        for jy in range(ny):
            at = pl.multiple_of(lax.rem(place[1] + jy, ny) * size, size)
            copies.append(
                pltpu.make_async_copy(
                    rows.at[panel, pl.ds(at, size), :], blocks.at[jy], sems.at[nx + jy]
                )
            )
        for copy in copies:
            copy.start()
        for jx in range(nx):
            copies[jx].wait()
            high, low = halves(strips[jx])
            span = slice(jx * 128, (jx + 1) * 128)
            right[0:depth, span] = high
            right[depth : 2 * depth, span] = low
            right[2 * depth : 3 * depth, span] = high
        for jy in range(ny):
            copies[nx + jy].wait()
            high, low = halves(blocks[jy])
            left[:, 0:depth] = high
            left[:, depth : 2 * depth] = high
            left[:, 2 * depth : 3 * depth] = low
            value = jnp.dot(left[...], right[...], preferred_element_type=F32)
            for jx in range(nx):
                block = value[:, jx * 128 : (jx + 1) * 128]
                first, second = (jx, jy) if by_column else (jy, jx)
                span = slice(second * size, (second + 1) * size)
                if has_received:
                    outs[first][span, :] = block + received[first, span, :]
                else:
                    outs[0][first, span, :] = block

    return kernel


def products(place, panel, rows, cols, received, by_column, nx, ny):
    kernel = product_kernel(panel, by_column, received is not None, nx, ny)
    _, size, depth = rows.shape
    first = nx if by_column else ny
    if received is None:
        shapes = jax.ShapeDtypeStruct((first, size, 128), F32)
        args = (place, rows, cols)
    else:
        shapes = [jax.ShapeDtypeStruct((size, 128), F32)] * first
        args = (place, rows, cols, received)
    return pl.pallas_call(
        kernel,
        out_shape=shapes,
        in_specs=[SMEM, FAR, FAR] + [pl.BlockSpec()] * (len(args) - 3),
        scratch_shapes=[
            pltpu.VMEM((size // ny, 3 * depth), BF16),
            pltpu.VMEM((3 * depth, nx * 128), BF16),
            pltpu.VMEM((nx, depth, 128), F32),
            pltpu.VMEM((ny, size // ny, depth), F32),
            pltpu.SemaphoreType.DMA((nx + ny,)),
        ],
        compiler_params=pltpu.CompilerParams(vmem_limit_bytes=16 << 20),
        cost_estimate=pl.CostEstimate(
            flops=6 * size * depth * nx * 128, transcendentals=0, bytes_accessed=6 << 20
        ),
    )(*args)


def pack_kernel(place, inverses, across, out):
    at = pl.multiple_of(place[0] * 256 + place[2] * 128, 128)
    strip_of_coupling = across[:, pl.ds(at, 128)]
    strip_of_second = inverses[1, :, pl.ds(at, 128)]
    nz = out.shape[0]
    for z in range(nz):
        out[z, :, 0:128] = strip_of_coupling
        out[z, :, 128:256] = strip_of_second
        for panel in range(2):
            pieces = [inverses[panel, :, y * 256 + z * 32 : y * 256 + z * 32 + 32] for y in range(4)]
            out[z, :, 256 + panel * 128 : 384 + panel * 128] = jnp.concatenate(pieces, axis=1)


def couple_kernel(tiles, out):
    out[...] = lax.dot_general(
        tiles[:, 0:128],
        tiles[:, 256:384],
        (((0,), (0,)), ((), ())),
        precision=EXACT,
        preferred_element_type=F32,
    )


def chain_kernel(tiles, part0, got1, got2, got3, out):
    total = (part0[...] + got1[256:384, :]) + (got2[256:384, :] + got3[256:384, :])
    out[...] = jnp.dot(tiles[:, 128:256], total, precision=EXACT, preferred_element_type=F32)


def gather_sums_kernel(a, b, c, d, rider, own, *outs):
    size = own.shape[0]
    for j, out in enumerate((own,) + outs):
        span = slice(j * size, (j + 1) * size)
        out[0:size, :] = (a[span, :] + b[span, :]) + (c[span, :] + d[span, :])
        if j:
            out[size:, :] = rider[...]


def gather_sums(parts, rider, count):
    size = parts[0].shape[0] // count
    longer = jax.ShapeDtypeStruct((size + rider.shape[0], 128), F32)
    return pl.pallas_call(
        gather_sums_kernel,
        out_shape=[jax.ShapeDtypeStruct((size, 128), F32)] + [longer] * (count - 1),
        compiler_params=SMALL,
    )(*parts, rider)


def interleave_kernel(a0, a1, a2, a3, b0, b1, b2, b3, part, out, mix):
    size = a0.shape[0]
    low = (a0[...] + a1[0:size, :]) + (a2[0:size, :] + a3[0:size, :])
    high = (b0[...] + b1[0:size, :]) + (b2[0:size, :] + b3[0:size, :])
    for z in range(out.shape[0]):
        out[z, 0:32, :] = low[z * 32 : (z + 1) * 32, :]
        out[z, 32:64, :] = high[z * 32 : (z + 1) * 32, :]
    mix[...] = (part[...] + b1[size:, :]) + (b2[size:, :] + b3[size:, :])


def apply_kernel(place, tiles, mix0, mix1, rest0, rest1, rest2, rest3, out, first, second):
    ny = 4
    for step, rest in enumerate((rest0, rest1, rest2, rest3)):
        at = pl.multiple_of(lax.rem(place[1] + ny - step, ny) * 32, 32)
        first[pl.ds(at, 32), :] = rest[0:32, :]
        second[pl.ds(at, 32), :] = rest[32:64, :]
    mix = mix0[...] + mix1[...]
    low = jnp.dot(tiles[:, 256:384], first[...], precision=EXACT, preferred_element_type=F32)
    high = jnp.dot(tiles[:, 384:512], second[...], precision=EXACT, preferred_element_type=F32)
    high = high - jnp.dot(mix, first[...], precision=EXACT, preferred_element_type=F32)
    for z in range(out.shape[0]):
        out[z, 0:32, :] = low[z * 32 : (z + 1) * 32, :]
        out[z, 32:64, :] = high[z * 32 : (z + 1) * 32, :]


def steps(panel_rows, solved, right_side, coupling, inverses):
    nx, ny, nz, nc = (lax.axis_size(a) for a in ("x", "y", "z", "core"))
    x, y, core = lax.axis_index("x"), lax.axis_index("y"), lax.axis_index("core")
    panel_rows = pltpu.with_memory_space_constraint(panel_rows, pltpu.HBM)
    solved = pltpu.with_memory_space_constraint(solved, pltpu.HBM)
    own = jnp.stack([x, y, core]).astype(jnp.int32)
    other = jnp.stack([x, y, 1 - core]).astype(jnp.int32)

    to_partner0 = products(other, 0, panel_rows, solved, None, True, nx, ny)
    from_partner0 = shift(to_partner0, "core", 1, nc)
    to_partner1 = products(other, 1, panel_rows, solved, None, False, nx, ny)
    from_partner1 = shift(to_partner1, "core", 1, nc)
    blocks0 = products(own, 0, panel_rows, solved, from_partner0, True, nx, ny)
    got0 = [blocks0[0]] + [shift(blocks0[j], "x", j, nx) for j in range(1, nx)]
    blocks1 = products(own, 1, panel_rows, solved, from_partner1, False, nx, ny)
    got1 = [blocks1[0]] + [shift(blocks1[j], "y", j, ny) for j in range(1, ny)]

    packed = pl.pallas_call(
        pack_kernel,
        out_shape=jax.ShapeDtypeStruct((nz, 32, 512), F32),
        in_specs=[SMEM, pl.BlockSpec(), pl.BlockSpec()],
        compiler_params=SMALL,
    )(own, inverses, coupling.T)
    tiles = lax.all_to_all(packed, "z", 0, 0, tiled=True).reshape(nz * 32, 512)
    coupled = pl.pallas_call(
        couple_kernel, out_shape=jax.ShapeDtypeStruct((128, 128), F32), compiler_params=SMALL
    )(tiles)

    sums0 = gather_sums(got0, coupled, ny)
    again0 = [sums0[0]] + [shift(sums0[j], "y", j, ny) for j in range(1, ny)]
    chained = pl.pallas_call(
        chain_kernel, out_shape=jax.ShapeDtypeStruct((256, 128), F32), compiler_params=SMALL
    )(tiles, coupled, *again0[1:])
    sums1 = gather_sums(got1, chained, nx)
    again1 = [sums1[0]] + [shift(sums1[j], "x", j, nx) for j in range(1, nx)]
    by_z, mix = pl.pallas_call(
        interleave_kernel,
        out_shape=(
            jax.ShapeDtypeStruct((nz, 64, 128), F32),
            jax.ShapeDtypeStruct((256, 128), F32),
        ),
        compiler_params=SMALL,
    )(*again0, *again1, chained)
    old = lax.all_to_all(by_z, "z", 0, 0, tiled=True).sum(axis=0)
    mix_of_partner = shift(mix, "core", 1, nc)
    rest = right_side.reshape(64, 128) - old

    rests = [rest] + [shift(rest, "y", j, ny) for j in range(1, ny)]
    solved_part = pl.pallas_call(
        apply_kernel,
        out_shape=jax.ShapeDtypeStruct((nz, 64, 128), F32),
        in_specs=[SMEM] + [pl.BlockSpec()] * 7,
        scratch_shapes=[pltpu.VMEM((128, 128), F32), pltpu.VMEM((128, 128), F32)],
        compiler_params=SMALL,
    )(own, tiles, mix, mix_of_partner, *rests)
    panels = lax.all_to_all(solved_part, "z", 0, 0, tiled=True).sum(axis=0)
    return panels.reshape(right_side.shape)


def solution(mesh):
    finer = Mesh(mesh.devices.reshape(4, 8, 4, 2), AXES)
    prow, pcol = ("y", "z"), ("x", "core")
    return jax.shard_map(
        steps,
        mesh=finer,
        in_specs=(
            P(None, None, AXES),
            P(AXES, None),
            P(None, prow, pcol),
            P(None, prow),
            P(None, prow, None),
        ),
        out_specs=P(None, prow, pcol),
        check_vma=False,
    )
```

```python
import jax
import jax.numpy as jnp
from jax import lax
from jax.experimental import pallas as pl
from jax.experimental.pallas import tpu as pltpu
from jax.sharding import Mesh
from jax.sharding import PartitionSpec as P


AXES = ("y", "z", "x", "core")
F32 = jnp.float32
BF16 = jnp.bfloat16
EXACT = lax.Precision.HIGHEST
SMEM = pl.BlockSpec(memory_space=pltpu.SMEM)
FAR = pl.BlockSpec(memory_space=pltpu.HBM)
SMALL = pltpu.CompilerParams(vmem_limit_bytes=6 << 20)


def far(value):
    return pltpu.with_memory_space_constraint(value, pltpu.HBM)


def shift(value, axis, step, size):
    return lax.ppermute(value, axis, [(i, (i + step) % size) for i in range(size)])


def halves(value):
    high = value.astype(BF16)
    return high, (value - high.astype(F32)).astype(BF16)


def product_kernel(panel, by_column, has_received, nx, ny):
    def kernel(place, rows, cols, *refs):
        received = refs[0] if has_received else None
        outs = refs[1:-4] if has_received else refs[:-4]
        left, right, blocks, sems = refs[-4:]
        depth = cols.shape[0]
        size = blocks.shape[1]
        copies = []
        for jy in range(ny):
            at = pl.multiple_of(lax.rem(place[1] + jy, ny) * size, size)
            copies.append(
                pltpu.make_async_copy(
                    rows.at[panel, pl.ds(at, size), :], blocks.at[jy], sems.at[jy]
                )
            )
        for copy in copies:
            copy.start()
        for jx in range(nx):
            at = lax.rem(place[0] + jx, nx) * 256 + place[2] * 128
            high, low = halves(cols[:, pl.ds(pl.multiple_of(at, 128), 128)])
            span = slice(jx * 128, (jx + 1) * 128)
            right[0:depth, span] = high
            right[depth : 2 * depth, span] = low
            right[2 * depth : 3 * depth, span] = high
        for jy in range(ny):
            copies[jy].wait()
            high, low = halves(blocks[jy])
            left[:, 0:depth] = high
            left[:, depth : 2 * depth] = high
            left[:, 2 * depth : 3 * depth] = low
            value = jnp.dot(left[...], right[...], preferred_element_type=F32)
            for jx in range(nx):
                block = value[:, jx * 128 : (jx + 1) * 128]
                first, second = (jx, jy) if by_column else (jy, jx)
                span = slice(second * size, (second + 1) * size)
                if has_received:
                    outs[first][span, :] = block + received[first, span, :]
                else:
                    outs[0][first, span, :] = block

    return kernel


def products(place, panel, rows, cols, received, by_column, nx, ny):
    kernel = product_kernel(panel, by_column, received is not None, nx, ny)
    _, size, depth = rows.shape
    first = nx if by_column else ny
    if received is None:
        shapes = jax.ShapeDtypeStruct((first, size, 128), F32)
        args = (place, rows, cols)
    else:
        shapes = [jax.ShapeDtypeStruct((size, 128), F32)] * first
        args = (place, rows, cols, received)
    return pl.pallas_call(
        kernel,
        out_shape=shapes,
        in_specs=[SMEM, FAR] + [pl.BlockSpec()] * (len(args) - 2),
        scratch_shapes=[
            pltpu.VMEM((size // ny, 3 * depth), BF16),
            pltpu.VMEM((3 * depth, nx * 128), BF16),
            pltpu.VMEM((ny, size // ny, depth), F32),
            pltpu.SemaphoreType.DMA((ny,)),
        ],
        compiler_params=pltpu.CompilerParams(vmem_limit_bytes=12 << 20),
        cost_estimate=pl.CostEstimate(
            flops=6 * size * depth * nx * 128, transcendentals=0, bytes_accessed=6 << 20
        ),
    )(*args)


def pack_kernel(place, inverses, across, out):
    at = pl.multiple_of(place[0] * 256 + place[2] * 128, 128)
    strip_of_coupling = across[:, pl.ds(at, 128)]
    strip_of_second = inverses[1, :, pl.ds(at, 128)]
    nz = out.shape[0]
    for z in range(nz):
        out[z, :, 0:128] = strip_of_coupling
        out[z, :, 128:256] = strip_of_second
        for panel in range(2):
            pieces = [inverses[panel, :, y * 256 + z * 32 : y * 256 + z * 32 + 32] for y in range(4)]
            out[z, :, 256 + panel * 128 : 384 + panel * 128] = jnp.concatenate(pieces, axis=1)


def couple_kernel(tiles, out):
    out[...] = lax.dot_general(
        tiles[:, 0:128],
        tiles[:, 256:384],
        (((0,), (0,)), ((), ())),
        precision=EXACT,
        preferred_element_type=F32,
    )


def chain_kernel(tiles, part0, part1, part2, part3, out):
    total = (part0[...] + part1[...]) + (part2[...] + part3[...])
    out[...] = jnp.dot(tiles[:, 128:256], total, precision=EXACT, preferred_element_type=F32)


def sum_kernel(a, b, out):
    out[...] = a[...] + b[...]


def gather_sums_kernel(a, b, c, d, *outs):
    size = outs[0].shape[0]
    for j, out in enumerate(outs):
        span = slice(j * size, (j + 1) * size)
        out[...] = (a[span, :] + b[span, :]) + (c[span, :] + d[span, :])


def gather_sums(parts, count):
    size = parts[0].shape[0] // count
    return pl.pallas_call(
        gather_sums_kernel,
        out_shape=[jax.ShapeDtypeStruct((size, 128), F32)] * count,
        compiler_params=SMALL,
    )(*parts)


def interleave_kernel(a0, a1, a2, a3, b0, b1, b2, b3, out):
    low = (a0[...] + a1[...]) + (a2[...] + a3[...])
    high = (b0[...] + b1[...]) + (b2[...] + b3[...])
    for z in range(out.shape[0]):
        out[z, 0:32, :] = low[z * 32 : (z + 1) * 32, :]
        out[z, 32:64, :] = high[z * 32 : (z + 1) * 32, :]


def apply_kernel(place, tiles, mix0, mix1, mix2, mix3, rest0, rest1, rest2, rest3, out, first, second):
    ny = 4
    for step, rest in enumerate((rest0, rest1, rest2, rest3)):
        at = pl.multiple_of(lax.rem(place[1] + ny - step, ny) * 32, 32)
        first[pl.ds(at, 32), :] = rest[0:32, :]
        second[pl.ds(at, 32), :] = rest[32:64, :]
    mix = (mix0[...] + mix1[...]) + (mix2[...] + mix3[...])
    low = jnp.dot(tiles[:, 256:384], first[...], precision=EXACT, preferred_element_type=F32)
    high = jnp.dot(tiles[:, 384:512], second[...], precision=EXACT, preferred_element_type=F32)
    high = high - jnp.dot(mix, first[...], precision=EXACT, preferred_element_type=F32)
    for z in range(out.shape[0]):
        out[z, 0:32, :] = low[z * 32 : (z + 1) * 32, :]
        out[z, 32:64, :] = high[z * 32 : (z + 1) * 32, :]


def steps(panel_rows, solved, right_side, coupling, inverses):
    nx, ny, nz, nc = (lax.axis_size(a) for a in ("x", "y", "z", "core"))
    x, y, core = lax.axis_index("x"), lax.axis_index("y"), lax.axis_index("core")
    panel_rows = far(panel_rows)
    own = jnp.stack([x, y, core]).astype(jnp.int32)
    other = jnp.stack([x, y, 1 - core]).astype(jnp.int32)

    packed = pl.pallas_call(
        pack_kernel,
        out_shape=jax.ShapeDtypeStruct((nz, 32, 512), F32),
        in_specs=[SMEM, pl.BlockSpec(), pl.BlockSpec()],
        compiler_params=SMALL,
    )(own, inverses, coupling.T)
    tiles = lax.all_to_all(packed, "z", 0, 0, tiled=True).reshape(nz * 32, 512)

    to_partner0 = products(other, 0, panel_rows, solved, None, True, nx, ny)
    from_partner0 = shift(to_partner0, "core", 1, nc)
    to_partner1 = products(other, 1, panel_rows, solved, None, False, nx, ny)
    from_partner1 = shift(to_partner1, "core", 1, nc)
    blocks0 = products(own, 0, panel_rows, solved, from_partner0, True, nx, ny)
    got0 = [blocks0[0]] + [shift(blocks0[j], "x", j, nx) for j in range(1, nx)]
    blocks1 = products(own, 1, panel_rows, solved, from_partner1, False, nx, ny)
    got1 = [blocks1[0]] + [shift(blocks1[j], "y", j, ny) for j in range(1, ny)]

    coupled = pl.pallas_call(
        couple_kernel, out_shape=jax.ShapeDtypeStruct((128, 128), F32), compiler_params=SMALL
    )(tiles)
    coupled_all = [coupled] + [shift(coupled, "y", j, ny) for j in range(1, ny)]
    chained = pl.pallas_call(
        chain_kernel, out_shape=jax.ShapeDtypeStruct((256, 128), F32), compiler_params=SMALL
    )(tiles, *coupled_all)
    mix = pl.pallas_call(
        sum_kernel, out_shape=jax.ShapeDtypeStruct((256, 128), F32), compiler_params=SMALL
    )(chained, shift(chained, "core", 1, nc))
    mixes = [mix] + [shift(mix, "x", j, nx) for j in range(1, nx)]

    sums0 = gather_sums(got0, ny)
    again0 = [sums0[0]] + [shift(sums0[j], "y", j, ny) for j in range(1, ny)]
    sums1 = gather_sums(got1, nx)
    again1 = [sums1[0]] + [shift(sums1[j], "x", j, nx) for j in range(1, nx)]
    by_z = pl.pallas_call(
        interleave_kernel, out_shape=jax.ShapeDtypeStruct((nz, 64, 128), F32), compiler_params=SMALL
    )(*again0, *again1)
    old = lax.all_to_all(by_z, "z", 0, 0, tiled=True).sum(axis=0)
    rest = right_side.reshape(64, 128) - old

    rests = [rest] + [shift(rest, "y", j, ny) for j in range(1, ny)]
    solved_part = pl.pallas_call(
        apply_kernel,
        out_shape=jax.ShapeDtypeStruct((nz, 64, 128), F32),
        in_specs=[SMEM] + [pl.BlockSpec()] * 9,
        scratch_shapes=[pltpu.VMEM((128, 128), F32), pltpu.VMEM((128, 128), F32)],
        compiler_params=SMALL,
    )(own, tiles, *mixes, *rests)
    panels = lax.all_to_all(solved_part, "z", 0, 0, tiled=True).sum(axis=0)
    return panels.reshape(right_side.shape)


def solution(mesh):
    finer = Mesh(mesh.devices.reshape(4, 8, 4, 2), AXES)
    prow, pcol = ("y", "z"), ("x", "core")
    return jax.shard_map(
        steps,
        mesh=finer,
        in_specs=(
            P(None, None, AXES),
            P(AXES, None),
            P(None, prow, pcol),
            P(None, prow),
            P(None, prow, None),
        ),
        out_specs=P(None, prow, pcol),
        check_vma=False,
    )
```

```python
import jax
import jax.numpy as jnp
from jax import lax
from jax.experimental import pallas as pl
from jax.experimental.pallas import tpu as pltpu
from jax.sharding import Mesh
from jax.sharding import PartitionSpec as P


AXES = ("y", "z", "x", "core")
F32 = jnp.float32
BF16 = jnp.bfloat16
EXACT = lax.Precision.HIGHEST
SMEM = pl.BlockSpec(memory_space=pltpu.SMEM)
FAR = pl.BlockSpec(memory_space=pltpu.HBM)
PRODUCT = pltpu.CompilerParams(vmem_limit_bytes=16 << 20)
ORDER = pl.BlockSpec(memory_space=pl.ANY)
SMALL = pltpu.CompilerParams(vmem_limit_bytes=6 << 20)


def far(value):
    return pltpu.with_memory_space_constraint(value, pltpu.HBM)


def shift(value, axis, step, size):
    return lax.ppermute(value, axis, [(i, (i + step) % size) for i in range(size)])


def halves(value):
    high = value.astype(BF16)
    return high, (value - high.astype(F32)).astype(BF16)


def split_columns(place, cols, right, nx):
    depth = cols.shape[0]
    for jx in range(nx):
        at = lax.rem(place[0] + jx, nx) * 256 + place[2] * 128
        high, low = halves(cols[:, pl.ds(pl.multiple_of(at, 128), 128)])
        span = slice(jx * 128, (jx + 1) * 128)
        right[0:depth, span] = high
        right[depth : 2 * depth, span] = low
        right[2 * depth : 3 * depth, span] = high


def multiply(block, left, right):
    depth = block.shape[1]
    high, low = halves(block)
    left[:, 0:depth] = high
    left[:, depth : 2 * depth] = high
    left[:, 2 * depth : 3 * depth] = low
    return jnp.dot(left[...], right[...], preferred_element_type=F32)


def rows_at(place, jy, ny, size):
    return pl.ds(pl.multiple_of(lax.rem(place[1] + jy, ny) * size, size), size)


def product_kernel(panel, by_column, has_received, nx, ny):
    def kernel(place, rows, cols, *refs):
        received = refs[0] if has_received else None
        outs = refs[1:-2] if has_received else refs[:-2]
        left, right = refs[-2:]
        size = left.shape[0]
        split_columns(place, cols, right, nx)
        for jy in range(ny):
            value = multiply(rows[panel, rows_at(place, jy, ny, size), :], left, right)
            for jx in range(nx):
                block = value[:, jx * 128 : (jx + 1) * 128]
                first, second = (jx, jy) if by_column else (jy, jx)
                span = slice(second * size, (second + 1) * size)
                if has_received:
                    outs[first][span, :] = block + received[first, span, :]
                else:
                    outs[0][first, span, :] = block

    return kernel


def first_kernel(nx, ny):
    def kernel(place, far_rows, far_cols, out, rows, cols, left, right, sems):
        size = left.shape[0]
        load_cols = pltpu.make_async_copy(far_cols, cols, sems.at[0])
        load_cols.start()
        loads = []
        for panel in range(2):
            for jy in range(ny):
                at = rows_at(place, jy, ny, size)
                loads.append(
                    pltpu.make_async_copy(
                        far_rows.at[panel, at, :], rows.at[panel, at, :], sems.at[1 + panel * ny + jy]
                    )
                )
        for load in loads:
            load.start()
        load_cols.wait()
        split_columns(place, cols, right, nx)
        for jy in range(ny):
            loads[jy].wait()
            value = multiply(rows[0, rows_at(place, jy, ny, size), :], left, right)
            for jx in range(nx):
                out[jx, jy * size : (jy + 1) * size, :] = value[:, jx * 128 : (jx + 1) * 128]
        for load in loads[ny:]:
            load.wait()

    return kernel


def product_scratch(size, depth, nx, ny):
    return [pltpu.VMEM((size // ny, 3 * depth), BF16), pltpu.VMEM((3 * depth, nx * 128), BF16)]


def product_cost(size, depth, nx):
    return pl.CostEstimate(
        flops=6 * size * depth * nx * 128, transcendentals=0, bytes_accessed=6 << 20
    )


def first_products(place, rows, cols, nx, ny):
    _, size, depth = rows.shape
    return pl.pallas_call(
        first_kernel(nx, ny),
        out_shape=(
            jax.ShapeDtypeStruct((nx, size, 128), F32),
            jax.ShapeDtypeStruct(rows.shape, F32),
            jax.ShapeDtypeStruct(cols.shape, F32),
        ),
        in_specs=[SMEM, FAR, FAR],
        scratch_shapes=product_scratch(size, depth, nx, ny)
        + [pltpu.SemaphoreType.DMA((1 + 2 * ny,))],
        compiler_params=PRODUCT,
        cost_estimate=product_cost(size, depth, nx),
    )(place, far(rows), far(cols))


def products(place, panel, rows, cols, received, by_column, nx, ny):
    kernel = product_kernel(panel, by_column, received is not None, nx, ny)
    _, size, depth = rows.shape
    first = nx if by_column else ny
    if received is None:
        shapes = jax.ShapeDtypeStruct((first, size, 128), F32)
        args = (place, rows, cols)
    else:
        shapes = [jax.ShapeDtypeStruct((size, 128), F32)] * first
        args = (place, rows, cols, received)
    return pl.pallas_call(
        kernel,
        out_shape=shapes,
        in_specs=[SMEM] + [pl.BlockSpec()] * (len(args) - 1),
        scratch_shapes=product_scratch(size, depth, nx, ny),
        compiler_params=PRODUCT,
        cost_estimate=product_cost(size, depth, nx),
    )(*args)


def pack_kernel(place, inverses, across, out):
    at = pl.multiple_of(place[0] * 256 + place[2] * 128, 128)
    strip_of_coupling = across[:, pl.ds(at, 128)]
    strip_of_second = inverses[1, :, pl.ds(at, 128)]
    nz = out.shape[0]
    for z in range(nz):
        out[z, :, 0:128] = strip_of_coupling
        out[z, :, 128:256] = strip_of_second
        for panel in range(2):
            pieces = [inverses[panel, :, y * 256 + z * 32 : y * 256 + z * 32 + 32] for y in range(4)]
            out[z, :, 256 + panel * 128 : 384 + panel * 128] = jnp.concatenate(pieces, axis=1)


def couple_kernel(tiles, out):
    out[...] = lax.dot_general(
        tiles[:, 0:128],
        tiles[:, 256:384],
        (((0,), (0,)), ((), ())),
        precision=EXACT,
        preferred_element_type=F32,
    )


def chain_kernel(tiles, part0, part1, part2, part3, out):
    total = (part0[...] + part1[...]) + (part2[...] + part3[...])
    out[...] = jnp.dot(tiles[:, 128:256], total, precision=EXACT, preferred_element_type=F32)


def sum_kernel(a, b, out):
    out[...] = a[...] + b[...]


def gather_sums_kernel(a, b, c, d, after, *outs):
    size = outs[0].shape[0]
    for j, out in enumerate(outs):
        span = slice(j * size, (j + 1) * size)
        out[...] = (a[span, :] + b[span, :]) + (c[span, :] + d[span, :])


def gather_sums(parts, after, count):
    size = parts[0].shape[0] // count
    return pl.pallas_call(
        gather_sums_kernel,
        out_shape=[jax.ShapeDtypeStruct((size, 128), F32)] * count,
        in_specs=[pl.BlockSpec()] * len(parts) + [ORDER],
        compiler_params=SMALL,
    )(*parts, after)


def interleave_kernel(a0, a1, a2, a3, b0, b1, b2, b3, out):
    low = (a0[...] + a1[...]) + (a2[...] + a3[...])
    high = (b0[...] + b1[...]) + (b2[...] + b3[...])
    for z in range(out.shape[0]):
        out[z, 0:32, :] = low[z * 32 : (z + 1) * 32, :]
        out[z, 32:64, :] = high[z * 32 : (z + 1) * 32, :]


def apply_kernel(place, tiles, mix0, mix1, mix2, mix3, rest0, rest1, rest2, rest3, out, first, second):
    ny = 4
    for step, rest in enumerate((rest0, rest1, rest2, rest3)):
        at = pl.multiple_of(lax.rem(place[1] + ny - step, ny) * 32, 32)
        first[pl.ds(at, 32), :] = rest[0:32, :]
        second[pl.ds(at, 32), :] = rest[32:64, :]
    mix = (mix0[...] + mix1[...]) + (mix2[...] + mix3[...])
    low = jnp.dot(tiles[:, 256:384], first[...], precision=EXACT, preferred_element_type=F32)
    high = jnp.dot(tiles[:, 384:512], second[...], precision=EXACT, preferred_element_type=F32)
    high = high - jnp.dot(mix, first[...], precision=EXACT, preferred_element_type=F32)
    for z in range(out.shape[0]):
        out[z, 0:32, :] = low[z * 32 : (z + 1) * 32, :]
        out[z, 32:64, :] = high[z * 32 : (z + 1) * 32, :]


def steps(panel_rows, solved, right_side, coupling, inverses):
    nx, ny, nz, nc = (lax.axis_size(a) for a in ("x", "y", "z", "core"))
    x, y, core = lax.axis_index("x"), lax.axis_index("y"), lax.axis_index("core")
    own = jnp.stack([x, y, core]).astype(jnp.int32)
    other = jnp.stack([x, y, 1 - core]).astype(jnp.int32)

    to_partner0, panel_rows, solved = first_products(other, panel_rows, solved, nx, ny)
    from_partner0 = shift(to_partner0, "core", 1, nc)
    to_partner1 = products(other, 1, panel_rows, solved, None, False, nx, ny)
    from_partner1 = shift(to_partner1, "core", 1, nc)
    blocks0 = products(own, 0, panel_rows, solved, from_partner0, True, nx, ny)
    got0 = [blocks0[0]] + [shift(blocks0[j], "x", j, nx) for j in range(1, nx)]
    blocks1 = products(own, 1, panel_rows, solved, from_partner1, False, nx, ny)
    got1 = [blocks1[0]] + [shift(blocks1[j], "y", j, ny) for j in range(1, ny)]

    packed = pl.pallas_call(
        pack_kernel,
        out_shape=jax.ShapeDtypeStruct((nz, 32, 512), F32),
        in_specs=[SMEM, pl.BlockSpec(), pl.BlockSpec()],
        compiler_params=SMALL,
    )(own, inverses, coupling.T)
    tiles = lax.all_to_all(packed, "z", 0, 0, tiled=True).reshape(nz * 32, 512)

    coupled = pl.pallas_call(
        couple_kernel, out_shape=jax.ShapeDtypeStruct((128, 128), F32), compiler_params=SMALL
    )(tiles)
    coupled_all = [coupled] + [shift(coupled, "y", j, ny) for j in range(1, ny)]
    chained = pl.pallas_call(
        chain_kernel, out_shape=jax.ShapeDtypeStruct((256, 128), F32), compiler_params=SMALL
    )(tiles, *coupled_all)
    mix = pl.pallas_call(
        sum_kernel, out_shape=jax.ShapeDtypeStruct((256, 128), F32), compiler_params=SMALL
    )(chained, shift(chained, "core", 1, nc))
    mixes = [mix] + [shift(mix, "x", j, nx) for j in range(1, nx)]

    sums0 = gather_sums(got0, coupled, ny)
    again0 = [sums0[0]] + [shift(sums0[j], "y", j, ny) for j in range(1, ny)]
    sums1 = gather_sums(got1, coupled, nx)
    again1 = [sums1[0]] + [shift(sums1[j], "x", j, nx) for j in range(1, nx)]
    by_z = pl.pallas_call(
        interleave_kernel,
        out_shape=jax.ShapeDtypeStruct((nz, 64, 128), F32),
        compiler_params=SMALL,
    )(*again0, *again1)
    old = lax.all_to_all(by_z, "z", 0, 0, tiled=True).sum(axis=0)
    rest = right_side.reshape(64, 128) - old

    rests = [rest] + [shift(rest, "y", j, ny) for j in range(1, ny)]
    solved_part = pl.pallas_call(
        apply_kernel,
        out_shape=jax.ShapeDtypeStruct((nz, 64, 128), F32),
        in_specs=[SMEM] + [pl.BlockSpec()] * 9,
        scratch_shapes=[pltpu.VMEM((128, 128), F32), pltpu.VMEM((128, 128), F32)],
        compiler_params=SMALL,
    )(own, tiles, *mixes, *rests)
    panels = lax.all_to_all(solved_part, "z", 0, 0, tiled=True).sum(axis=0)
    return panels.reshape(right_side.shape)


def solution(mesh):
    finer = Mesh(mesh.devices.reshape(4, 8, 4, 2), AXES)
    prow, pcol = ("y", "z"), ("x", "core")
    return jax.shard_map(
        steps,
        mesh=finer,
        in_specs=(
            P(None, None, AXES),
            P(AXES, None),
            P(None, prow, pcol),
            P(None, prow),
            P(None, prow, None),
        ),
        out_specs=P(None, prow, pcol),
        check_vma=False,
    )
```

```python
import jax
import jax.numpy as jnp
from jax import lax
from jax.experimental import pallas as pl
from jax.experimental.pallas import tpu as pltpu
from jax.sharding import Mesh
from jax.sharding import PartitionSpec as P


AXES = ("y", "z", "x", "core")
F32 = jnp.float32
BF16 = jnp.bfloat16
EXACT = lax.Precision.HIGHEST
SMEM = pl.BlockSpec(memory_space=pltpu.SMEM)
FAR = pl.BlockSpec(memory_space=pltpu.HBM)
PRODUCT = pltpu.CompilerParams(vmem_limit_bytes=16 << 20)
ORDER = pl.BlockSpec(memory_space=pl.ANY)
SMALL = pltpu.CompilerParams(vmem_limit_bytes=6 << 20)


def far(value):
    return pltpu.with_memory_space_constraint(value, pltpu.HBM)


def shift(value, axis, step, size):
    return lax.ppermute(value, axis, [(i, (i + step) % size) for i in range(size)])


def halves(value):
    high = value.astype(BF16)
    return high, (value - high.astype(F32)).astype(BF16)


def split_columns(place, cols, right, nx):
    depth = cols.shape[0]
    for jx in range(nx):
        at = lax.rem(place[0] + jx, nx) * 256 + place[2] * 128
        high, low = halves(cols[:, pl.ds(pl.multiple_of(at, 128), 128)])
        span = slice(jx * 128, (jx + 1) * 128)
        right[0:depth, span] = high
        right[depth : 2 * depth, span] = low
        right[2 * depth : 3 * depth, span] = high


def multiply(block, left, right):
    depth = block.shape[1]
    high, low = halves(block)
    left[:, 0:depth] = high
    left[:, depth : 2 * depth] = high
    left[:, 2 * depth : 3 * depth] = low
    return jnp.dot(left[...], right[...], preferred_element_type=F32)


def rows_at(place, jy, ny, size):
    return pl.ds(pl.multiple_of(lax.rem(place[1] + jy, ny) * size, size), size)


def product_kernel(panel, by_column, has_received, nx, ny):
    def kernel(place, rows, cols, *refs):
        received = refs[0] if has_received else None
        outs = refs[1:-2] if has_received else refs[:-2]
        left, right = refs[-2:]
        size = left.shape[0]
        split_columns(place, cols, right, nx)
        for jy in range(ny):
            value = multiply(rows[panel, rows_at(place, jy, ny, size), :], left, right)
            for jx in range(nx):
                block = value[:, jx * 128 : (jx + 1) * 128]
                first, second = (jx, jy) if by_column else (jy, jx)
                span = slice(second * size, (second + 1) * size)
                if has_received:
                    outs[first][span, :] = block + received[first, span, :]
                else:
                    outs[0][first, span, :] = block

    return kernel


def first_kernel(nx, ny):
    def kernel(place, far_rows, far_cols, out, rows, cols, left, right, sems):
        size = left.shape[0]
        part = cols.shape[0] // ny
        first_loads = []
        for k in range(ny):
            at = slice(k * part, (k + 1) * part)
            first_loads.append(
                pltpu.make_async_copy(far_cols.at[at, :], cols.at[at, :], sems.at[2 * ny + k])
            )
        loads = []
        for panel in range(2):
            for jy in range(ny):
                at = rows_at(place, jy, ny, size)
                loads.append(
                    pltpu.make_async_copy(
                        far_rows.at[panel, at, :], rows.at[panel, at, :], sems.at[panel * ny + jy]
                    )
                )
        for load in first_loads + loads:
            load.start()
        for load in first_loads:
            load.wait()
        split_columns(place, cols, right, nx)
        for jy in range(ny):
            loads[jy].wait()
            value = multiply(rows[0, rows_at(place, jy, ny, size), :], left, right)
            for jx in range(nx):
                out[jx, jy * size : (jy + 1) * size, :] = value[:, jx * 128 : (jx + 1) * 128]
        for load in loads[ny:]:
            load.wait()

    return kernel


def product_scratch(size, depth, nx, ny):
    return [pltpu.VMEM((size // ny, 3 * depth), BF16), pltpu.VMEM((3 * depth, nx * 128), BF16)]


def product_cost(size, depth, nx):
    return pl.CostEstimate(
        flops=6 * size * depth * nx * 128, transcendentals=0, bytes_accessed=6 << 20
    )


def first_products(place, rows, cols, nx, ny):
    _, size, depth = rows.shape
    return pl.pallas_call(
        first_kernel(nx, ny),
        out_shape=(
            jax.ShapeDtypeStruct((nx, size, 128), F32),
            jax.ShapeDtypeStruct(rows.shape, F32),
            jax.ShapeDtypeStruct(cols.shape, F32),
        ),
        in_specs=[SMEM, FAR, FAR],
        scratch_shapes=product_scratch(size, depth, nx, ny)
        + [pltpu.SemaphoreType.DMA((3 * ny,))],
        compiler_params=PRODUCT,
        cost_estimate=product_cost(size, depth, nx),
    )(place, far(rows), far(cols))


def products(place, panel, rows, cols, received, by_column, nx, ny):
    kernel = product_kernel(panel, by_column, received is not None, nx, ny)
    _, size, depth = rows.shape
    first = nx if by_column else ny
    if received is None:
        shapes = jax.ShapeDtypeStruct((first, size, 128), F32)
        args = (place, rows, cols)
    else:
        shapes = [jax.ShapeDtypeStruct((size, 128), F32)] * first
        args = (place, rows, cols, received)
    return pl.pallas_call(
        kernel,
        out_shape=shapes,
        in_specs=[SMEM] + [pl.BlockSpec()] * (len(args) - 1),
        scratch_shapes=product_scratch(size, depth, nx, ny),
        compiler_params=PRODUCT,
        cost_estimate=product_cost(size, depth, nx),
    )(*args)


def pack_kernel(place, inverses, across, out):
    at = pl.multiple_of(place[0] * 256 + place[2] * 128, 128)
    strip_of_coupling = across[:, pl.ds(at, 128)]
    strip_of_second = inverses[1, :, pl.ds(at, 128)]
    nz = out.shape[0]
    for z in range(nz):
        out[z, :, 0:128] = strip_of_coupling
        out[z, :, 128:256] = strip_of_second
        for panel in range(2):
            pieces = [inverses[panel, :, y * 256 + z * 32 : y * 256 + z * 32 + 32] for y in range(4)]
            out[z, :, 256 + panel * 128 : 384 + panel * 128] = jnp.concatenate(pieces, axis=1)


def couple_kernel(tiles, out):
    out[...] = lax.dot_general(
        tiles[:, 0:128],
        tiles[:, 256:384],
        (((0,), (0,)), ((), ())),
        precision=EXACT,
        preferred_element_type=F32,
    )


def chain_kernel(tiles, part0, got1, got2, got3, out):
    at = got1.shape[0] - 128
    total = (part0[...] + got1[at:, :]) + (got2[at:, :] + got3[at:, :])
    out[...] = jnp.dot(tiles[:, 128:256], total, precision=EXACT, preferred_element_type=F32)


def sum_kernel(a, b, out):
    out[...] = a[...] + b[...]


def gather_sums_kernel(a, b, c, d, rider, own, *outs):
    size = own.shape[0]
    for j, out in enumerate((own,) + outs):
        span = slice(j * size, (j + 1) * size)
        out[0:size, :] = (a[span, :] + b[span, :]) + (c[span, :] + d[span, :])
        if j and out.shape[0] > size:
            out[size:, :] = rider[...]


def gather_sums(parts, rider, count, carried):
    size = parts[0].shape[0] // count
    longer = jax.ShapeDtypeStruct((size + (rider.shape[0] if carried else 0), 128), F32)
    return pl.pallas_call(
        gather_sums_kernel,
        out_shape=[jax.ShapeDtypeStruct((size, 128), F32)] + [longer] * (count - 1),
        in_specs=[pl.BlockSpec()] * len(parts) + [pl.BlockSpec() if carried else ORDER],
        compiler_params=SMALL,
    )(*parts, rider)


def interleave_kernel(a0, a1, a2, a3, b0, b1, b2, b3, out):
    size = a0.shape[0]
    low = (a0[...] + a1[0:size, :]) + (a2[0:size, :] + a3[0:size, :])
    high = (b0[...] + b1[...]) + (b2[...] + b3[...])
    for z in range(out.shape[0]):
        out[z, 0:32, :] = low[z * 32 : (z + 1) * 32, :]
        out[z, 32:64, :] = high[z * 32 : (z + 1) * 32, :]


def apply_kernel(place, tiles, mix0, mix1, mix2, mix3, rest0, rest1, rest2, rest3, out, first, second):
    ny = 4
    for step, rest in enumerate((rest0, rest1, rest2, rest3)):
        at = pl.multiple_of(lax.rem(place[1] + ny - step, ny) * 32, 32)
        first[pl.ds(at, 32), :] = rest[0:32, :]
        second[pl.ds(at, 32), :] = rest[32:64, :]
    mix = (mix0[...] + mix1[...]) + (mix2[...] + mix3[...])
    low = jnp.dot(tiles[:, 256:384], first[...], precision=EXACT, preferred_element_type=F32)
    high = jnp.dot(tiles[:, 384:512], second[...], precision=EXACT, preferred_element_type=F32)
    high = high - jnp.dot(mix, first[...], precision=EXACT, preferred_element_type=F32)
    for z in range(out.shape[0]):
        out[z, 0:32, :] = low[z * 32 : (z + 1) * 32, :]
        out[z, 32:64, :] = high[z * 32 : (z + 1) * 32, :]


def steps(panel_rows, solved, right_side, coupling, inverses):
    nx, ny, nz, nc = (lax.axis_size(a) for a in ("x", "y", "z", "core"))
    x, y, core = lax.axis_index("x"), lax.axis_index("y"), lax.axis_index("core")
    own = jnp.stack([x, y, core]).astype(jnp.int32)
    other = jnp.stack([x, y, 1 - core]).astype(jnp.int32)

    to_partner0, panel_rows, solved = first_products(other, panel_rows, solved, nx, ny)
    from_partner0 = shift(to_partner0, "core", 1, nc)
    to_partner1 = products(other, 1, panel_rows, solved, None, False, nx, ny)
    from_partner1 = shift(to_partner1, "core", 1, nc)
    blocks0 = products(own, 0, panel_rows, solved, from_partner0, True, nx, ny)
    got0 = [blocks0[0]] + [shift(blocks0[j], "x", j, nx) for j in range(1, nx)]
    blocks1 = products(own, 1, panel_rows, solved, from_partner1, False, nx, ny)
    got1 = [blocks1[0]] + [shift(blocks1[j], "y", j, ny) for j in range(1, ny)]

    packed = pl.pallas_call(
        pack_kernel,
        out_shape=jax.ShapeDtypeStruct((nz, 32, 512), F32),
        in_specs=[SMEM, pl.BlockSpec(), pl.BlockSpec()],
        compiler_params=SMALL,
    )(own, inverses, coupling.T)
    tiles = lax.all_to_all(packed, "z", 0, 0, tiled=True).reshape(nz * 32, 512)

    coupled = pl.pallas_call(
        couple_kernel, out_shape=jax.ShapeDtypeStruct((128, 128), F32), compiler_params=SMALL
    )(tiles)
    sums0 = gather_sums(got0, coupled, ny, True)
    again0 = [sums0[0]] + [shift(sums0[j], "y", j, ny) for j in range(1, ny)]
    sums1 = gather_sums(got1, coupled, nx, False)
    again1 = [sums1[0]] + [shift(sums1[j], "x", j, nx) for j in range(1, nx)]
    by_z = pl.pallas_call(
        interleave_kernel,
        out_shape=jax.ShapeDtypeStruct((nz, 64, 128), F32),
        compiler_params=SMALL,
    )(*again0, *again1)
    chained = pl.pallas_call(
        chain_kernel, out_shape=jax.ShapeDtypeStruct((256, 128), F32), compiler_params=SMALL
    )(tiles, coupled, *again0[1:])
    mix = pl.pallas_call(
        sum_kernel, out_shape=jax.ShapeDtypeStruct((256, 128), F32), compiler_params=SMALL
    )(chained, shift(chained, "core", 1, nc))
    mixes = [mix] + [shift(mix, "x", j, nx) for j in range(1, nx)]
    old = lax.all_to_all(by_z, "z", 0, 0, tiled=True).sum(axis=0)
    rest = right_side.reshape(64, 128) - old

    rests = [rest] + [shift(rest, "y", j, ny) for j in range(1, ny)]
    solved_part = pl.pallas_call(
        apply_kernel,
        out_shape=jax.ShapeDtypeStruct((nz, 64, 128), F32),
        in_specs=[SMEM] + [pl.BlockSpec()] * 9,
        scratch_shapes=[pltpu.VMEM((128, 128), F32), pltpu.VMEM((128, 128), F32)],
        compiler_params=SMALL,
    )(own, tiles, *mixes, *rests)
    panels = lax.all_to_all(solved_part, "z", 0, 0, tiled=True).sum(axis=0)
    return panels.reshape(right_side.shape)


def solution(mesh):
    finer = Mesh(mesh.devices.reshape(4, 8, 4, 2), AXES)
    prow, pcol = ("y", "z"), ("x", "core")
    return jax.shard_map(
        steps,
        mesh=finer,
        in_specs=(
            P(None, None, AXES),
            P(AXES, None),
            P(None, prow, pcol),
            P(None, prow),
            P(None, prow, None),
        ),
        out_specs=P(None, prow, pcol),
        check_vma=False,
    )
```

```python
import jax
import jax.numpy as jnp
from jax import lax
from jax.experimental import pallas as pl
from jax.experimental.pallas import tpu as pltpu
from jax.sharding import Mesh
from jax.sharding import PartitionSpec as P


AXES = ("y", "z", "x", "core")
F32 = jnp.float32
BF16 = jnp.bfloat16
EXACT = lax.Precision.HIGHEST
SMEM = pl.BlockSpec(memory_space=pltpu.SMEM)
FAR = pl.BlockSpec(memory_space=pltpu.HBM)
PRODUCT = pltpu.CompilerParams(vmem_limit_bytes=16 << 20)
ORDER = pl.BlockSpec(memory_space=pl.ANY)
SMALL = pltpu.CompilerParams(vmem_limit_bytes=6 << 20)


def far(value):
    return pltpu.with_memory_space_constraint(value, pltpu.HBM)


def shift(value, axis, step, size):
    return lax.ppermute(value, axis, [(i, (i + step) % size) for i in range(size)])


def halves(value):
    high = value.astype(BF16)
    return high, (value - high.astype(F32)).astype(BF16)


def split_columns(place, cols, right, nx):
    depth = cols.shape[0]
    for jx in range(nx):
        at = lax.rem(place[0] + jx, nx) * 256 + place[2] * 128
        high, low = halves(cols[:, pl.ds(pl.multiple_of(at, 128), 128)])
        span = slice(jx * 128, (jx + 1) * 128)
        right[0:depth, span] = high
        right[depth : 2 * depth, span] = low
        right[2 * depth : 3 * depth, span] = high


def multiply(block, left, right):
    depth = block.shape[1]
    high, low = halves(block)
    left[:, 0:depth] = high
    left[:, depth : 2 * depth] = high
    left[:, 2 * depth : 3 * depth] = low
    return jnp.dot(left[...], right[...], preferred_element_type=F32)


def rows_at(place, jy, ny, size):
    return pl.ds(pl.multiple_of(lax.rem(place[1] + jy, ny) * size, size), size)


def product_kernel(panel, by_column, has_received, nx, ny):
    def kernel(place, rows, cols, *refs):
        received = refs[0] if has_received else None
        outs = refs[1:-2] if has_received else refs[:-2]
        left, right = refs[-2:]
        size = left.shape[0]
        split_columns(place, cols, right, nx)
        for jy in range(ny):
            value = multiply(rows[panel, rows_at(place, jy, ny, size), :], left, right)
            for jx in range(nx):
                block = value[:, jx * 128 : (jx + 1) * 128]
                first, second = (jx, jy) if by_column else (jy, jx)
                span = slice(second * size, (second + 1) * size)
                if has_received:
                    outs[first][span, :] = block + received[first, span, :]
                else:
                    outs[0][first, span, :] = block

    return kernel


def first_kernel(nx, ny):
    def kernel(place, far_rows, far_cols, out, rows, cols, left, right, sems):
        size = left.shape[0]
        part = cols.shape[0] // ny
        first_loads = []
        for k in range(ny):
            at = slice(k * part, (k + 1) * part)
            first_loads.append(
                pltpu.make_async_copy(far_cols.at[at, :], cols.at[at, :], sems.at[2 * ny + k])
            )
        loads = []
        for panel in range(2):
            for jy in range(ny):
                at = rows_at(place, jy, ny, size)
                loads.append(
                    pltpu.make_async_copy(
                        far_rows.at[panel, at, :], rows.at[panel, at, :], sems.at[panel * ny + jy]
                    )
                )
        for load in first_loads + loads[:ny]:
            load.start()
        for load in first_loads:
            load.wait()
        split_columns(place, cols, right, nx)
        for jy in range(ny):
            loads[jy].wait()
            if jy == 0:
                for load in loads[ny:]:
                    load.start()
            value = multiply(rows[0, rows_at(place, jy, ny, size), :], left, right)
            for jx in range(nx):
                out[jx, jy * size : (jy + 1) * size, :] = value[:, jx * 128 : (jx + 1) * 128]
        for load in loads[ny:]:
            load.wait()

    return kernel


def product_scratch(size, depth, nx, ny):
    return [pltpu.VMEM((size // ny, 3 * depth), BF16), pltpu.VMEM((3 * depth, nx * 128), BF16)]


def product_cost(size, depth, nx):
    return pl.CostEstimate(
        flops=6 * size * depth * nx * 128, transcendentals=0, bytes_accessed=6 << 20
    )


def first_products(place, rows, cols, nx, ny):
    _, size, depth = rows.shape
    return pl.pallas_call(
        first_kernel(nx, ny),
        out_shape=(
            jax.ShapeDtypeStruct((nx, size, 128), F32),
            jax.ShapeDtypeStruct(rows.shape, F32),
            jax.ShapeDtypeStruct(cols.shape, F32),
        ),
        in_specs=[SMEM, FAR, FAR],
        scratch_shapes=product_scratch(size, depth, nx, ny)
        + [pltpu.SemaphoreType.DMA((3 * ny,))],
        compiler_params=PRODUCT,
        cost_estimate=product_cost(size, depth, nx),
    )(place, far(rows), far(cols))


def products(place, panel, rows, cols, received, by_column, nx, ny):
    kernel = product_kernel(panel, by_column, received is not None, nx, ny)
    _, size, depth = rows.shape
    first = nx if by_column else ny
    if received is None:
        shapes = jax.ShapeDtypeStruct((first, size, 128), F32)
        args = (place, rows, cols)
    else:
        shapes = [jax.ShapeDtypeStruct((size, 128), F32)] * first
        args = (place, rows, cols, received)
    return pl.pallas_call(
        kernel,
        out_shape=shapes,
        in_specs=[SMEM] + [pl.BlockSpec()] * (len(args) - 1),
        scratch_shapes=product_scratch(size, depth, nx, ny),
        compiler_params=PRODUCT,
        cost_estimate=product_cost(size, depth, nx),
    )(*args)


def pack_kernel(place, inverses, across, out, late):
    at = pl.multiple_of(place[0] * 256 + place[2] * 128, 128)
    strip_of_coupling = across[:, pl.ds(at, 128)]
    strip_of_second = inverses[1, :, pl.ds(at, 128)]
    for z in range(out.shape[0]):
        out[z, :, 0:128] = strip_of_coupling
        out[z, :, 128:256] = strip_of_second
        slabs = []
        for panel in range(2):
            pieces = [inverses[panel, :, y * 256 + z * 32 : y * 256 + z * 32 + 32] for y in range(4)]
            slabs.append(jnp.concatenate(pieces, axis=1))
        out[z, :, 256:384] = slabs[0]
        late[z] = slabs[1]


def couple_kernel(tiles, out):
    out[...] = lax.dot_general(
        tiles[:, 0:128],
        tiles[:, 256:384],
        (((0,), (0,)), ((), ())),
        precision=EXACT,
        preferred_element_type=F32,
    )


def chain_kernel(tiles, part0, got1, got2, got3, out):
    at = got1.shape[0] - 128
    total = (part0[...] + got1[at:, :]) + (got2[at:, :] + got3[at:, :])
    out[...] = jnp.dot(tiles[:, 128:256], total, precision=EXACT, preferred_element_type=F32)


def sum_kernel(a, b, out):
    out[...] = a[...] + b[...]


def gather_sums_kernel(a, b, c, d, rider, own, *outs):
    size = own.shape[0]
    for j, out in enumerate((own,) + outs):
        span = slice(j * size, (j + 1) * size)
        out[0:size, :] = (a[span, :] + b[span, :]) + (c[span, :] + d[span, :])
        if j and out.shape[0] > size:
            out[size:, :] = rider[...]


def gather_sums(parts, rider, count, carried):
    size = parts[0].shape[0] // count
    longer = jax.ShapeDtypeStruct((size + (rider.shape[0] if carried else 0), 128), F32)
    return pl.pallas_call(
        gather_sums_kernel,
        out_shape=[jax.ShapeDtypeStruct((size, 128), F32)] + [longer] * (count - 1),
        in_specs=[pl.BlockSpec()] * len(parts) + [pl.BlockSpec() if carried else ORDER],
        compiler_params=SMALL,
    )(*parts, rider)


def interleave_kernel(a0, a1, a2, a3, b0, b1, b2, b3, late, out):
    size = a0.shape[0]
    low = (a0[...] + a1[0:size, :]) + (a2[0:size, :] + a3[0:size, :])
    high = (b0[...] + b1[...]) + (b2[...] + b3[...])
    for z in range(out.shape[0]):
        out[z, 0:32, :] = low[z * 32 : (z + 1) * 32, :]
        out[z, 32:64, :] = high[z * 32 : (z + 1) * 32, :]
        out[z, 64:96, :] = late[z]


def rest_kernel(got, right_side, out):
    total = [got[z, 0:64, :] for z in range(got.shape[0])]
    while len(total) > 1:
        total = [a + b for a, b in zip(total[::2], total[1::2])]
    out[...] = right_side[...] - total[0]


def apply_kernel(place, tiles, got, mix0, mix1, mix2, mix3, rest0, rest1, rest2, rest3, out, first, second):
    ny = 4
    nz = out.shape[0]
    for step, rest in enumerate((rest0, rest1, rest2, rest3)):
        at = pl.multiple_of(lax.rem(place[1] + ny - step, ny) * 32, 32)
        first[pl.ds(at, 32), :] = rest[0:32, :]
        second[pl.ds(at, 32), :] = rest[32:64, :]
    mix = (mix0[...] + mix1[...]) + (mix2[...] + mix3[...])
    slab = got[:, 64:96, :].reshape(nz * 32, 128)
    low = jnp.dot(tiles[:, 256:384], first[...], precision=EXACT, preferred_element_type=F32)
    high = jnp.dot(slab, second[...], precision=EXACT, preferred_element_type=F32)
    high = high - jnp.dot(mix, first[...], precision=EXACT, preferred_element_type=F32)
    for z in range(nz):
        out[z, 0:32, :] = low[z * 32 : (z + 1) * 32, :]
        out[z, 32:64, :] = high[z * 32 : (z + 1) * 32, :]


def steps(panel_rows, solved, right_side, coupling, inverses):
    nx, ny, nz, nc = (lax.axis_size(a) for a in ("x", "y", "z", "core"))
    x, y, core = lax.axis_index("x"), lax.axis_index("y"), lax.axis_index("core")
    own = jnp.stack([x, y, core]).astype(jnp.int32)
    other = jnp.stack([x, y, 1 - core]).astype(jnp.int32)

    to_partner0, panel_rows, solved = first_products(other, panel_rows, solved, nx, ny)
    from_partner0 = shift(to_partner0, "core", 1, nc)
    to_partner1 = products(other, 1, panel_rows, solved, None, False, nx, ny)
    from_partner1 = shift(to_partner1, "core", 1, nc)
    blocks0 = products(own, 0, panel_rows, solved, from_partner0, True, nx, ny)
    got0 = [blocks0[0]] + [shift(blocks0[j], "x", j, nx) for j in range(1, nx)]
    blocks1 = products(own, 1, panel_rows, solved, from_partner1, False, nx, ny)
    got1 = [blocks1[0]] + [shift(blocks1[j], "y", j, ny) for j in range(1, ny)]

    packed, late = pl.pallas_call(
        pack_kernel,
        out_shape=(
            jax.ShapeDtypeStruct((nz, 32, 384), F32),
            jax.ShapeDtypeStruct((nz, 32, 128), F32),
        ),
        in_specs=[SMEM, pl.BlockSpec(), pl.BlockSpec()],
        compiler_params=SMALL,
    )(own, inverses, coupling.T)
    tiles = lax.all_to_all(packed, "z", 0, 0, tiled=True).reshape(nz * 32, 384)

    coupled = pl.pallas_call(
        couple_kernel, out_shape=jax.ShapeDtypeStruct((128, 128), F32), compiler_params=SMALL
    )(tiles)
    sums0 = gather_sums(got0, coupled, ny, True)
    again0 = [sums0[0]] + [shift(sums0[j], "y", j, ny) for j in range(1, ny)]
    sums1 = gather_sums(got1, coupled, nx, False)
    again1 = [sums1[0]] + [shift(sums1[j], "x", j, nx) for j in range(1, nx)]
    by_z = pl.pallas_call(
        interleave_kernel,
        out_shape=jax.ShapeDtypeStruct((nz, 96, 128), F32),
        compiler_params=SMALL,
    )(*again0, *again1, late)
    chained = pl.pallas_call(
        chain_kernel, out_shape=jax.ShapeDtypeStruct((256, 128), F32), compiler_params=SMALL
    )(tiles, coupled, *again0[1:])
    mix = pl.pallas_call(
        sum_kernel, out_shape=jax.ShapeDtypeStruct((256, 128), F32), compiler_params=SMALL
    )(chained, shift(chained, "core", 1, nc))
    mixes = [mix] + [shift(mix, "x", j, nx) for j in range(1, nx)]
    by_source = lax.all_to_all(by_z, "z", 0, 0, tiled=True)
    rest = pl.pallas_call(
        rest_kernel, out_shape=jax.ShapeDtypeStruct((64, 128), F32), compiler_params=SMALL
    )(by_source, right_side.reshape(64, 128))

    rests = [rest] + [shift(rest, "y", j, ny) for j in range(1, ny)]
    solved_part = pl.pallas_call(
        apply_kernel,
        out_shape=jax.ShapeDtypeStruct((nz, 64, 128), F32),
        in_specs=[SMEM] + [pl.BlockSpec()] * 10,
        scratch_shapes=[pltpu.VMEM((128, 128), F32), pltpu.VMEM((128, 128), F32)],
        compiler_params=SMALL,
    )(own, tiles, by_source, *mixes, *rests)
    panels = lax.all_to_all(solved_part, "z", 0, 0, tiled=True).sum(axis=0)
    return panels.reshape(right_side.shape)


def solution(mesh):
    finer = Mesh(mesh.devices.reshape(4, 8, 4, 2), AXES)
    prow, pcol = ("y", "z"), ("x", "core")
    return jax.shard_map(
        steps,
        mesh=finer,
        in_specs=(
            P(None, None, AXES),
            P(AXES, None),
            P(None, prow, pcol),
            P(None, prow),
            P(None, prow, None),
        ),
        out_specs=P(None, prow, pcol),
        check_vma=False,
    )
```

```python
import jax
import jax.numpy as jnp
from jax import lax
from jax.experimental import pallas as pl
from jax.experimental.pallas import tpu as pltpu
from jax.sharding import Mesh
from jax.sharding import PartitionSpec as P


AXES = ("y", "z", "x", "core")
F32 = jnp.float32
BF16 = jnp.bfloat16
EXACT = lax.Precision.HIGHEST
SMEM = pl.BlockSpec(memory_space=pltpu.SMEM)
FAR = pl.BlockSpec(memory_space=pltpu.HBM)
PRODUCT = pltpu.CompilerParams(vmem_limit_bytes=16 << 20)
SMALL = pltpu.CompilerParams(vmem_limit_bytes=6 << 20)


def far(value):
    return pltpu.with_memory_space_constraint(value, pltpu.HBM)


def shift(value, axis, step, size):
    return lax.ppermute(value, axis, [(i, (i + step) % size) for i in range(size)])


def halves(value):
    high = value.astype(BF16)
    return high, (value - high.astype(F32)).astype(BF16)


def split_columns(place, cols, right, nx):
    depth = cols.shape[0]
    for jx in range(nx):
        at = lax.rem(place[0] + jx, nx) * 256 + place[2] * 128
        high, low = halves(cols[:, pl.ds(pl.multiple_of(at, 128), 128)])
        span = slice(jx * 128, (jx + 1) * 128)
        right[0:depth, span] = high
        right[depth : 2 * depth, span] = low
        right[2 * depth : 3 * depth, span] = high


def multiply(block, left, right):
    depth = block.shape[1]
    high, low = halves(block)
    left[:, 0:depth] = high
    left[:, depth : 2 * depth] = high
    left[:, 2 * depth : 3 * depth] = low
    return jnp.dot(left[...], right[...], preferred_element_type=F32)


def rows_at(place, jy, ny, size):
    return pl.ds(pl.multiple_of(lax.rem(place[1] + jy, ny) * size, size), size)


def product_kernel(panel, by_column, has_received, nx, ny):
    def kernel(place, rows, cols, *refs):
        received = refs[0] if has_received else None
        outs = refs[1:-2] if has_received else refs[:-2]
        left, right = refs[-2:]
        size = left.shape[0]
        split_columns(place, cols, right, nx)
        for jy in range(ny):
            value = multiply(rows[panel, rows_at(place, jy, ny, size), :], left, right)
            for jx in range(nx):
                block = value[:, jx * 128 : (jx + 1) * 128]
                first, second = (jx, jy) if by_column else (jy, jx)
                span = slice(second * size, (second + 1) * size)
                if has_received:
                    outs[first][span, :] = block + received[first, span, :]
                else:
                    outs[0][first, span, :] = block

    return kernel


def first_kernel(nx, ny):
    def kernel(place, far_rows, far_cols, out, rows, cols, left, right, sems):
        size = left.shape[0]
        part = cols.shape[0] // ny
        first_loads = []
        for k in range(ny):
            at = slice(k * part, (k + 1) * part)
            first_loads.append(
                pltpu.make_async_copy(far_cols.at[at, :], cols.at[at, :], sems.at[2 * ny + k])
            )
        loads = []
        for panel in range(2):
            for jy in range(ny):
                at = rows_at(place, jy, ny, size)
                loads.append(
                    pltpu.make_async_copy(
                        far_rows.at[panel, at, :], rows.at[panel, at, :], sems.at[panel * ny + jy]
                    )
                )
        for load in first_loads + loads[:ny]:
            load.start()
        for load in first_loads:
            load.wait()
        split_columns(place, cols, right, nx)
        for jy in range(ny):
            loads[jy].wait()
            if jy == 0:
                for load in loads[ny:]:
                    load.start()
            value = multiply(rows[0, rows_at(place, jy, ny, size), :], left, right)
            for jx in range(nx):
                out[jx, jy * size : (jy + 1) * size, :] = value[:, jx * 128 : (jx + 1) * 128]
        for load in loads[ny:]:
            load.wait()

    return kernel


def product_scratch(size, depth, nx, ny):
    return [pltpu.VMEM((size // ny, 3 * depth), BF16), pltpu.VMEM((3 * depth, nx * 128), BF16)]


def product_cost(size, depth, nx):
    return pl.CostEstimate(
        flops=6 * size * depth * nx * 128, transcendentals=0, bytes_accessed=6 << 20
    )


def first_products(place, rows, cols, nx, ny):
    _, size, depth = rows.shape
    return pl.pallas_call(
        first_kernel(nx, ny),
        out_shape=(
            jax.ShapeDtypeStruct((nx, size, 128), F32),
            jax.ShapeDtypeStruct(rows.shape, F32),
            jax.ShapeDtypeStruct(cols.shape, F32),
        ),
        in_specs=[SMEM, FAR, FAR],
        scratch_shapes=product_scratch(size, depth, nx, ny)
        + [pltpu.SemaphoreType.DMA((3 * ny,))],
        compiler_params=PRODUCT,
        cost_estimate=product_cost(size, depth, nx),
    )(place, far(rows), far(cols))


def products(place, panel, rows, cols, received, by_column, nx, ny):
    kernel = product_kernel(panel, by_column, received is not None, nx, ny)
    _, size, depth = rows.shape
    first = nx if by_column else ny
    if received is None:
        shapes = jax.ShapeDtypeStruct((first, size, 128), F32)
        args = (place, rows, cols)
    else:
        shapes = [jax.ShapeDtypeStruct((size, 128), F32)] * first
        args = (place, rows, cols, received)
    return pl.pallas_call(
        kernel,
        out_shape=shapes,
        in_specs=[SMEM] + [pl.BlockSpec()] * (len(args) - 1),
        scratch_shapes=product_scratch(size, depth, nx, ny),
        compiler_params=PRODUCT,
        cost_estimate=product_cost(size, depth, nx),
    )(*args)


def pack_kernel(place, inverses, across, out):
    at = pl.multiple_of(place[0] * 256 + place[2] * 128, 128)
    strip_of_coupling = across[:, pl.ds(at, 128)]
    strip_of_second = inverses[1, :, pl.ds(at, 128)]
    nz = out.shape[0]
    for z in range(nz):
        out[z, :, 0:128] = strip_of_coupling
        out[z, :, 128:256] = strip_of_second
        for panel in range(2):
            pieces = [inverses[panel, :, y * 256 + z * 32 : y * 256 + z * 32 + 32] for y in range(4)]
            out[z, :, 256 + panel * 128 : 384 + panel * 128] = jnp.concatenate(pieces, axis=1)


def couple_kernel(tiles, out):
    out[...] = lax.dot_general(
        tiles[:, 0:128],
        tiles[:, 256:384],
        (((0,), (0,)), ((), ())),
        precision=EXACT,
        preferred_element_type=F32,
    )


def chain_kernel(tiles, part0, part1, part2, part3, out):
    total = (part0[...] + part1[...]) + (part2[...] + part3[...])
    out[...] = jnp.dot(tiles[:, 128:256], total, precision=EXACT, preferred_element_type=F32)


def sum_kernel(a, b, out):
    out[...] = a[...] + b[...]


def gather_sums_kernel(a, b, c, d, *outs):
    size = outs[0].shape[0]
    for j, out in enumerate(outs):
        span = slice(j * size, (j + 1) * size)
        out[...] = (a[span, :] + b[span, :]) + (c[span, :] + d[span, :])


def gather_sums(parts, count):
    size = parts[0].shape[0] // count
    return pl.pallas_call(
        gather_sums_kernel,
        out_shape=[jax.ShapeDtypeStruct((size, 128), F32)] * count,
        compiler_params=SMALL,
    )(*parts)


def interleave_kernel(a0, a1, a2, a3, b0, b1, b2, b3, out):
    low = (a0[...] + a1[...]) + (a2[...] + a3[...])
    high = (b0[...] + b1[...]) + (b2[...] + b3[...])
    for z in range(out.shape[0]):
        out[z, 0:32, :] = low[z * 32 : (z + 1) * 32, :]
        out[z, 32:64, :] = high[z * 32 : (z + 1) * 32, :]


def apply_kernel(place, tiles, mix0, mix1, mix2, mix3, rest0, rest1, rest2, rest3, out, first, second):
    ny = 4
    for step, rest in enumerate((rest0, rest1, rest2, rest3)):
        at = pl.multiple_of(lax.rem(place[1] + ny - step, ny) * 32, 32)
        first[pl.ds(at, 32), :] = rest[0:32, :]
        second[pl.ds(at, 32), :] = rest[32:64, :]
    mix = (mix0[...] + mix1[...]) + (mix2[...] + mix3[...])
    low = jnp.dot(tiles[:, 256:384], first[...], precision=EXACT, preferred_element_type=F32)
    high = jnp.dot(tiles[:, 384:512], second[...], precision=EXACT, preferred_element_type=F32)
    high = high - jnp.dot(mix, first[...], precision=EXACT, preferred_element_type=F32)
    for z in range(out.shape[0]):
        out[z, 0:32, :] = low[z * 32 : (z + 1) * 32, :]
        out[z, 32:64, :] = high[z * 32 : (z + 1) * 32, :]


def steps(panel_rows, solved, right_side, coupling, inverses):
    nx, ny, nz, nc = (lax.axis_size(a) for a in ("x", "y", "z", "core"))
    x, y, core = lax.axis_index("x"), lax.axis_index("y"), lax.axis_index("core")
    own = jnp.stack([x, y, core]).astype(jnp.int32)
    other = jnp.stack([x, y, 1 - core]).astype(jnp.int32)

    to_partner0, panel_rows, solved = first_products(other, panel_rows, solved, nx, ny)
    from_partner0 = shift(to_partner0, "core", 1, nc)
    to_partner1 = products(other, 1, panel_rows, solved, None, False, nx, ny)
    from_partner1 = shift(to_partner1, "core", 1, nc)
    blocks0 = products(own, 0, panel_rows, solved, from_partner0, True, nx, ny)
    got0 = [blocks0[0]] + [shift(blocks0[j], "x", j, nx) for j in range(1, nx)]
    blocks1 = products(own, 1, panel_rows, solved, from_partner1, False, nx, ny)
    got1 = [blocks1[0]] + [shift(blocks1[j], "y", j, ny) for j in range(1, ny)]

    packed = pl.pallas_call(
        pack_kernel,
        out_shape=jax.ShapeDtypeStruct((nz, 32, 512), F32),
        in_specs=[SMEM, pl.BlockSpec(), pl.BlockSpec()],
        compiler_params=SMALL,
    )(own, inverses, coupling.T)
    tiles = lax.all_to_all(packed, "z", 0, 0, tiled=True).reshape(nz * 32, 512)

    coupled = pl.pallas_call(
        couple_kernel, out_shape=jax.ShapeDtypeStruct((128, 128), F32), compiler_params=SMALL
    )(tiles)
    coupled_all = [coupled] + [shift(coupled, "y", j, ny) for j in range(1, ny)]
    chained = pl.pallas_call(
        chain_kernel, out_shape=jax.ShapeDtypeStruct((256, 128), F32), compiler_params=SMALL
    )(tiles, *coupled_all)
    mix = pl.pallas_call(
        sum_kernel, out_shape=jax.ShapeDtypeStruct((256, 128), F32), compiler_params=SMALL
    )(chained, shift(chained, "core", 1, nc))
    mixes = [mix] + [shift(mix, "x", j, nx) for j in range(1, nx)]

    sums0 = gather_sums(got0, ny)
    again0 = [sums0[0]] + [shift(sums0[j], "y", j, ny) for j in range(1, ny)]
    sums1 = gather_sums(got1, nx)
    again1 = [sums1[0]] + [shift(sums1[j], "x", j, nx) for j in range(1, nx)]
    by_z = pl.pallas_call(
        interleave_kernel,
        out_shape=jax.ShapeDtypeStruct((nz, 64, 128), F32),
        compiler_params=SMALL,
    )(*again0, *again1)
    old = lax.all_to_all(by_z, "z", 0, 0, tiled=True).sum(axis=0)
    rest = right_side.reshape(64, 128) - old

    rests = [rest] + [shift(rest, "y", j, ny) for j in range(1, ny)]
    solved_part = pl.pallas_call(
        apply_kernel,
        out_shape=jax.ShapeDtypeStruct((nz, 64, 128), F32),
        in_specs=[SMEM] + [pl.BlockSpec()] * 9,
        scratch_shapes=[pltpu.VMEM((128, 128), F32), pltpu.VMEM((128, 128), F32)],
        compiler_params=SMALL,
    )(own, tiles, *mixes, *rests)
    panels = lax.all_to_all(solved_part, "z", 0, 0, tiled=True).sum(axis=0)
    return panels.reshape(right_side.shape)


def solution(mesh):
    finer = Mesh(mesh.devices.reshape(4, 8, 4, 2), AXES)
    prow, pcol = ("y", "z"), ("x", "core")
    return jax.shard_map(
        steps,
        mesh=finer,
        in_specs=(
            P(None, None, AXES),
            P(AXES, None),
            P(None, prow, pcol),
            P(None, prow),
            P(None, prow, None),
        ),
        out_specs=P(None, prow, pcol),
        check_vma=False,
    )
```

```python
import jax
import jax.numpy as jnp
from jax import lax
from jax.experimental import pallas as pl
from jax.experimental.pallas import tpu as pltpu
from jax.sharding import Mesh
from jax.sharding import PartitionSpec as P


AXES = ("y", "z", "x", "core")
F32 = jnp.float32
BF16 = jnp.bfloat16
EXACT = lax.Precision.HIGHEST
SMEM = pl.BlockSpec(memory_space=pltpu.SMEM)
FAR = pl.BlockSpec(memory_space=pltpu.HBM)
PRODUCT = pltpu.CompilerParams(vmem_limit_bytes=16 << 20)
ORDER = pl.BlockSpec(memory_space=pl.ANY)
SMALL = pltpu.CompilerParams(vmem_limit_bytes=6 << 20)


def far(value):
    return pltpu.with_memory_space_constraint(value, pltpu.HBM)


def shift(value, axis, step, size):
    return lax.ppermute(value, axis, [(i, (i + step) % size) for i in range(size)])


def halves(value):
    high = value.astype(BF16)
    return high, (value - high.astype(F32)).astype(BF16)


def split_columns(place, cols, right, nx):
    depth = cols.shape[0]
    for jx in range(nx):
        at = lax.rem(place[0] + jx, nx) * 256 + place[2] * 128
        high, low = halves(cols[:, pl.ds(pl.multiple_of(at, 128), 128)])
        span = slice(jx * 128, (jx + 1) * 128)
        right[0:depth, span] = high
        right[depth : 2 * depth, span] = low
        right[2 * depth : 3 * depth, span] = high


def multiply(block, left, right):
    depth = block.shape[1]
    high, low = halves(block)
    left[:, 0:depth] = high
    left[:, depth : 2 * depth] = high
    left[:, 2 * depth : 3 * depth] = low
    return jnp.dot(left[...], right[...], preferred_element_type=F32)


def rows_at(place, jy, ny, size):
    return pl.ds(pl.multiple_of(lax.rem(place[1] + jy, ny) * size, size), size)


def product_kernel(panel, by_column, has_received, nx, ny):
    def kernel(place, rows, cols, *refs):
        received = refs[0] if has_received else None
        outs = refs[1:-2] if has_received else refs[:-2]
        left, right = refs[-2:]
        size = left.shape[0]
        split_columns(place, cols, right, nx)
        for jy in range(ny):
            value = multiply(rows[panel, rows_at(place, jy, ny, size), :], left, right)
            for jx in range(nx):
                block = value[:, jx * 128 : (jx + 1) * 128]
                first, second = (jx, jy) if by_column else (jy, jx)
                span = slice(second * size, (second + 1) * size)
                if has_received:
                    outs[first][span, :] = block + received[first, span, :]
                else:
                    outs[0][first, span, :] = block

    return kernel


def first_kernel(nx, ny):
    def kernel(place, far_rows, far_cols, out, rows, cols, left, right, sems):
        size = left.shape[0]

        def strip(jx, core, sem):
            at = lax.rem(place[0] + jx, nx) * 256 + core * 128
            at = pl.ds(pl.multiple_of(at, 128), 128)
            return pltpu.make_async_copy(far_cols.at[:, at], cols.at[:, at], sems.at[sem])

        def block(panel, jy, sem):
            at = rows_at(place, jy, ny, size)
            return pltpu.make_async_copy(
                far_rows.at[panel, at, :], rows.at[panel, at, :], sems.at[sem]
            )

        strips = [strip(jx, place[2], jx) for jx in range(nx)]
        blocks = [block(0, jy, nx + jy) for jy in range(ny)]
        later = [strip(jx, 1 - place[2], nx + ny + jx) for jx in range(nx)]
        later += [block(1, jy, 2 * nx + ny + jy) for jy in range(ny)]
        for load in strips + blocks[:2]:
            load.start()
        for load in strips:
            load.wait()
        for load in blocks[2:]:
            load.start()
        split_columns(place, cols, right, nx)
        for jy in range(ny):
            blocks[jy].wait()
            if jy == 0:
                for load in later:
                    load.start()
            value = multiply(rows[0, rows_at(place, jy, ny, size), :], left, right)
            for jx in range(nx):
                out[jx, jy * size : (jy + 1) * size, :] = value[:, jx * 128 : (jx + 1) * 128]
        for load in later:
            load.wait()

    return kernel


def product_scratch(size, depth, nx, ny):
    return [pltpu.VMEM((size // ny, 3 * depth), BF16), pltpu.VMEM((3 * depth, nx * 128), BF16)]


def product_cost(size, depth, nx):
    return pl.CostEstimate(
        flops=6 * size * depth * nx * 128, transcendentals=0, bytes_accessed=6 << 20
    )


def first_products(place, rows, cols, nx, ny):
    _, size, depth = rows.shape
    return pl.pallas_call(
        first_kernel(nx, ny),
        out_shape=(
            jax.ShapeDtypeStruct((nx, size, 128), F32),
            jax.ShapeDtypeStruct(rows.shape, F32),
            jax.ShapeDtypeStruct(cols.shape, F32),
        ),
        in_specs=[SMEM, FAR, FAR],
        scratch_shapes=product_scratch(size, depth, nx, ny)
        + [pltpu.SemaphoreType.DMA((2 * nx + 2 * ny,))],
        compiler_params=PRODUCT,
        cost_estimate=product_cost(size, depth, nx),
    )(place, far(rows), far(cols))


def products(place, panel, rows, cols, received, by_column, nx, ny):
    kernel = product_kernel(panel, by_column, received is not None, nx, ny)
    _, size, depth = rows.shape
    first = nx if by_column else ny
    if received is None:
        shapes = jax.ShapeDtypeStruct((first, size, 128), F32)
        args = (place, rows, cols)
    else:
        shapes = [jax.ShapeDtypeStruct((size, 128), F32)] * first
        args = (place, rows, cols, received)
    return pl.pallas_call(
        kernel,
        out_shape=shapes,
        in_specs=[SMEM] + [pl.BlockSpec()] * (len(args) - 1),
        scratch_shapes=product_scratch(size, depth, nx, ny),
        compiler_params=PRODUCT,
        cost_estimate=product_cost(size, depth, nx),
    )(*args)


def pack_kernel(place, inverses, across, out):
    at = pl.multiple_of(place[0] * 256 + place[2] * 128, 128)
    strip_of_coupling = across[:, pl.ds(at, 128)]
    strip_of_second = inverses[1, :, pl.ds(at, 128)]
    nz = out.shape[0]
    for z in range(nz):
        out[z, :, 0:128] = strip_of_coupling
        out[z, :, 128:256] = strip_of_second
        for panel in range(2):
            pieces = [inverses[panel, :, y * 256 + z * 32 : y * 256 + z * 32 + 32] for y in range(4)]
            out[z, :, 256 + panel * 128 : 384 + panel * 128] = jnp.concatenate(pieces, axis=1)


def couple_kernel(tiles, out):
    out[...] = lax.dot_general(
        tiles[:, 0:128],
        tiles[:, 256:384],
        (((0,), (0,)), ((), ())),
        precision=EXACT,
        preferred_element_type=F32,
    )


def chain_kernel(tiles, part0, got1, got2, got3, out):
    at = got1.shape[0] - 128
    total = (part0[...] + got1[at:, :]) + (got2[at:, :] + got3[at:, :])
    out[...] = jnp.dot(tiles[:, 128:256], total, precision=EXACT, preferred_element_type=F32)


def sum_kernel(a, b, out):
    out[...] = a[...] + b[...]


def gather_sums_kernel(a, b, c, d, rider, own, *outs):
    size = own.shape[0]
    for j, out in enumerate((own,) + outs):
        span = slice(j * size, (j + 1) * size)
        out[0:size, :] = (a[span, :] + b[span, :]) + (c[span, :] + d[span, :])
        if j and out.shape[0] > size:
            out[size:, :] = rider[...]


def gather_sums(parts, rider, count, carried):
    size = parts[0].shape[0] // count
    longer = jax.ShapeDtypeStruct((size + (rider.shape[0] if carried else 0), 128), F32)
    return pl.pallas_call(
        gather_sums_kernel,
        out_shape=[jax.ShapeDtypeStruct((size, 128), F32)] + [longer] * (count - 1),
        in_specs=[pl.BlockSpec()] * len(parts) + [pl.BlockSpec() if carried else ORDER],
        compiler_params=SMALL,
    )(*parts, rider)


def interleave_kernel(a0, a1, a2, a3, b0, b1, b2, b3, out):
    size = a0.shape[0]
    low = (a0[...] + a1[0:size, :]) + (a2[0:size, :] + a3[0:size, :])
    high = (b0[...] + b1[...]) + (b2[...] + b3[...])
    for z in range(out.shape[0]):
        out[z, 0:32, :] = low[z * 32 : (z + 1) * 32, :]
        out[z, 32:64, :] = high[z * 32 : (z + 1) * 32, :]


def apply_kernel(place, tiles, mix0, mix1, mix2, mix3, rest0, rest1, rest2, rest3, out, first, second):
    ny = 4
    for step, rest in enumerate((rest0, rest1, rest2, rest3)):
        at = pl.multiple_of(lax.rem(place[1] + ny - step, ny) * 32, 32)
        first[pl.ds(at, 32), :] = rest[0:32, :]
        second[pl.ds(at, 32), :] = rest[32:64, :]
    mix = (mix0[...] + mix1[...]) + (mix2[...] + mix3[...])
    low = jnp.dot(tiles[:, 256:384], first[...], precision=EXACT, preferred_element_type=F32)
    high = jnp.dot(tiles[:, 384:512], second[...], precision=EXACT, preferred_element_type=F32)
    high = high - jnp.dot(mix, first[...], precision=EXACT, preferred_element_type=F32)
    for z in range(out.shape[0]):
        out[z, 0:32, :] = low[z * 32 : (z + 1) * 32, :]
        out[z, 32:64, :] = high[z * 32 : (z + 1) * 32, :]


def steps(panel_rows, solved, right_side, coupling, inverses):
    nx, ny, nz, nc = (lax.axis_size(a) for a in ("x", "y", "z", "core"))
    x, y, core = lax.axis_index("x"), lax.axis_index("y"), lax.axis_index("core")
    own = jnp.stack([x, y, core]).astype(jnp.int32)
    other = jnp.stack([x, y, 1 - core]).astype(jnp.int32)

    to_partner0, panel_rows, solved = first_products(other, panel_rows, solved, nx, ny)
    from_partner0 = shift(to_partner0, "core", 1, nc)
    to_partner1 = products(other, 1, panel_rows, solved, None, False, nx, ny)
    from_partner1 = shift(to_partner1, "core", 1, nc)
    blocks0 = products(own, 0, panel_rows, solved, from_partner0, True, nx, ny)
    got0 = [blocks0[0]] + [shift(blocks0[j], "x", j, nx) for j in range(1, nx)]
    blocks1 = products(own, 1, panel_rows, solved, from_partner1, False, nx, ny)
    got1 = [blocks1[0]] + [shift(blocks1[j], "y", j, ny) for j in range(1, ny)]

    packed = pl.pallas_call(
        pack_kernel,
        out_shape=jax.ShapeDtypeStruct((nz, 32, 512), F32),
        in_specs=[SMEM, pl.BlockSpec(), pl.BlockSpec()],
        compiler_params=SMALL,
    )(own, inverses, coupling.T)
    tiles = lax.all_to_all(packed, "z", 0, 0, tiled=True).reshape(nz * 32, 512)

    coupled = pl.pallas_call(
        couple_kernel, out_shape=jax.ShapeDtypeStruct((128, 128), F32), compiler_params=SMALL
    )(tiles)
    sums0 = gather_sums(got0, coupled, ny, True)
    again0 = [sums0[0]] + [shift(sums0[j], "y", j, ny) for j in range(1, ny)]
    sums1 = gather_sums(got1, coupled, nx, False)
    again1 = [sums1[0]] + [shift(sums1[j], "x", j, nx) for j in range(1, nx)]
    chained = pl.pallas_call(
        chain_kernel, out_shape=jax.ShapeDtypeStruct((256, 128), F32), compiler_params=SMALL
    )(tiles, coupled, *again0[1:])
    chained_of_partner = shift(chained, "core", 1, nc)
    by_z = pl.pallas_call(
        interleave_kernel,
        out_shape=jax.ShapeDtypeStruct((nz, 64, 128), F32),
        compiler_params=SMALL,
    )(*again0, *again1)
    mix = pl.pallas_call(
        sum_kernel, out_shape=jax.ShapeDtypeStruct((256, 128), F32), compiler_params=SMALL
    )(chained, chained_of_partner)
    mixes = [mix] + [shift(mix, "x", j, nx) for j in range(1, nx)]
    old = lax.all_to_all(by_z, "z", 0, 0, tiled=True).sum(axis=0)
    rest = right_side.reshape(64, 128) - old

    rests = [rest] + [shift(rest, "y", j, ny) for j in range(1, ny)]
    solved_part = pl.pallas_call(
        apply_kernel,
        out_shape=jax.ShapeDtypeStruct((nz, 64, 128), F32),
        in_specs=[SMEM] + [pl.BlockSpec()] * 9,
        scratch_shapes=[pltpu.VMEM((128, 128), F32), pltpu.VMEM((128, 128), F32)],
        compiler_params=SMALL,
    )(own, tiles, *mixes, *rests)
    panels = lax.all_to_all(solved_part, "z", 0, 0, tiled=True).sum(axis=0)
    return panels.reshape(right_side.shape)


def solution(mesh):
    finer = Mesh(mesh.devices.reshape(4, 8, 4, 2), AXES)
    prow, pcol = ("y", "z"), ("x", "core")
    return jax.shard_map(
        steps,
        mesh=finer,
        in_specs=(
            P(None, None, AXES),
            P(AXES, None),
            P(None, prow, pcol),
            P(None, prow),
            P(None, prow, None),
        ),
        out_specs=P(None, prow, pcol),
        check_vma=False,
    )
```

```python
import jax
import jax.numpy as jnp
from jax import lax
from jax.experimental import pallas as pl
from jax.experimental.pallas import tpu as pltpu
from jax.sharding import Mesh
from jax.sharding import PartitionSpec as P


AXES = ("y", "z", "x", "core")
F32 = jnp.float32
BF16 = jnp.bfloat16
EXACT = lax.Precision.HIGHEST
SMEM = pl.BlockSpec(memory_space=pltpu.SMEM)
FAR = pl.BlockSpec(memory_space=pltpu.HBM)
PRODUCT = pltpu.CompilerParams(vmem_limit_bytes=16 << 20)
ORDER = pl.BlockSpec(memory_space=pl.ANY)
SMALL = pltpu.CompilerParams(vmem_limit_bytes=6 << 20)


def far(value):
    return pltpu.with_memory_space_constraint(value, pltpu.HBM)


def shift(value, axis, step, size):
    return lax.ppermute(value, axis, [(i, (i + step) % size) for i in range(size)])


def halves(value):
    high = value.astype(BF16)
    return high, (value - high.astype(F32)).astype(BF16)


def split_columns(place, cols, right, nx):
    depth = cols.shape[0]
    for jx in range(nx):
        at = lax.rem(place[0] + jx, nx) * 256 + place[2] * 128
        high, low = halves(cols[:, pl.ds(pl.multiple_of(at, 128), 128)])
        span = slice(jx * 128, (jx + 1) * 128)
        right[0:depth, span] = high
        right[depth : 2 * depth, span] = low
        right[2 * depth : 3 * depth, span] = high


def pieces_of(group, ny, nz, tile_rows):
    block = tile_rows // ny
    end = block // nz
    return ((0, 0, block), (1, block - end, end)) if group == 0 else ((1, 0, block - end),)


def rows_of(group, ny, nz, tile_rows):
    return sum(piece[2] for piece in pieces_of(group, ny, nz, tile_rows))


def rows_at(place, jy, ny, tile_rows, first, count):
    block = tile_rows // ny
    at = lax.rem(place[1] + jy, ny) * block + first
    return pl.ds(pl.multiple_of(at, 32), count)


def multiply(place, rows, pieces, jy, ny, left, right):
    _, tile_rows, depth = rows.shape
    at = 0
    for panel, first, count in pieces:
        high, low = halves(rows[panel, rows_at(place, jy, ny, tile_rows, first, count), :])
        span = slice(at, at + count)
        left[span, 0:depth] = high
        left[span, depth : 2 * depth] = high
        left[span, 2 * depth : 3 * depth] = low
        at += count
    return jnp.dot(left[...], right[...], preferred_element_type=F32)


def product_kernel(pieces, by_column, has_received, nx, ny):
    def kernel(place, rows, cols, *refs):
        received = refs[0] if has_received else None
        outs = refs[1:-2] if has_received else refs[:-2]
        left, right = refs[-2:]
        size = left.shape[0]
        split_columns(place, cols, right, nx)
        for jy in range(ny):
            value = multiply(place, rows, pieces, jy, ny, left, right)
            for jx in range(nx):
                block = value[:, jx * 128 : (jx + 1) * 128]
                first, second = (jx, jy) if by_column else (jy, jx)
                span = slice(second * size, (second + 1) * size)
                if has_received:
                    outs[first][span, :] = block + received[first, span, :]
                else:
                    outs[0][first, span, :] = block

    return kernel


def first_kernel(pieces, rest, nx, ny):
    def kernel(place, far_rows, far_cols, out, rows, cols, left, right, sems):
        size = left.shape[0]
        tile_rows = rows.shape[1]

        def strip(jx, core, sem):
            at = lax.rem(place[0] + jx, nx) * 256 + core * 128
            at = pl.ds(pl.multiple_of(at, 128), 128)
            return pltpu.make_async_copy(far_cols.at[:, at], cols.at[:, at], sems.at[sem])

        def load_of(piece, jy, sem):
            panel, first, count = piece
            at = rows_at(place, jy, ny, tile_rows, first, count)
            return pltpu.make_async_copy(
                far_rows.at[panel, at, :], rows.at[panel, at, :], sems.at[sem]
            )

        strips = [strip(jx, place[2], jx) for jx in range(nx)]
        sem = nx
        blocks = []
        for jy in range(ny):
            blocks.append([load_of(piece, jy, sem + k) for k, piece in enumerate(pieces)])
            sem += len(pieces)
        later = [strip(jx, 1 - place[2], sem + jx) for jx in range(nx)]
        sem += nx
        for jy in range(ny):
            later += [load_of(piece, jy, sem + k) for k, piece in enumerate(rest)]
            sem += len(rest)
        for load in strips + blocks[0] + blocks[1]:
            load.start()
        for load in strips:
            load.wait()
        for block in blocks[2:]:
            for load in block:
                load.start()
        split_columns(place, cols, right, nx)
        for jy in range(ny):
            for load in blocks[jy]:
                load.wait()
            if jy == 0:
                for load in later:
                    load.start()
            value = multiply(place, rows, pieces, jy, ny, left, right)
            for jx in range(nx):
                out[jx, jy * size : (jy + 1) * size, :] = value[:, jx * 128 : (jx + 1) * 128]
        for load in later:
            load.wait()

    return kernel


def product_scratch(size, depth, nx):
    return [pltpu.VMEM((size, 3 * depth), BF16), pltpu.VMEM((3 * depth, nx * 128), BF16)]


def product_cost(size, depth, nx):
    return pl.CostEstimate(
        flops=6 * size * depth * nx * 128, transcendentals=0, bytes_accessed=6 << 20
    )


def first_products(place, rows, cols, nx, ny, nz):
    _, tile_rows, depth = rows.shape
    pieces, rest = (pieces_of(group, ny, nz, tile_rows) for group in (0, 1))
    size = rows_of(0, ny, nz, tile_rows)
    copies = 2 * nx + ny * (len(pieces) + len(rest))
    return pl.pallas_call(
        first_kernel(pieces, rest, nx, ny),
        out_shape=(
            jax.ShapeDtypeStruct((nx, ny * size, 128), F32),
            jax.ShapeDtypeStruct(rows.shape, F32),
            jax.ShapeDtypeStruct(cols.shape, F32),
        ),
        in_specs=[SMEM, FAR, FAR],
        scratch_shapes=product_scratch(size, depth, nx) + [pltpu.SemaphoreType.DMA((copies,))],
        compiler_params=PRODUCT,
        cost_estimate=product_cost(ny * size, depth, nx),
    )(place, far(rows), far(cols))


def products(place, group, rows, cols, received, by_column, nx, ny, nz):
    _, tile_rows, depth = rows.shape
    size = rows_of(group, ny, nz, tile_rows)
    pieces = pieces_of(group, ny, nz, tile_rows)
    kernel = product_kernel(pieces, by_column, received is not None, nx, ny)
    first, second = (nx, ny) if by_column else (ny, nx)
    if received is None:
        shapes = jax.ShapeDtypeStruct((first, second * size, 128), F32)
        args = (place, rows, cols)
    else:
        shapes = [jax.ShapeDtypeStruct((second * size, 128), F32)] * first
        args = (place, rows, cols, received)
    return pl.pallas_call(
        kernel,
        out_shape=shapes,
        in_specs=[SMEM] + [pl.BlockSpec()] * (len(args) - 1),
        scratch_shapes=product_scratch(size, depth, nx),
        compiler_params=PRODUCT,
        cost_estimate=product_cost(second * size, depth, nx),
    )(*args)


def pack_kernel(place, inverses, across, out):
    at = pl.multiple_of(place[0] * 256 + place[2] * 128, 128)
    strip_of_coupling = across[:, pl.ds(at, 128)]
    strip_of_second = inverses[1, :, pl.ds(at, 128)]
    nz = out.shape[0]
    for z in range(nz):
        out[z, :, 0:128] = strip_of_coupling
        out[z, :, 128:256] = strip_of_second
        for panel in range(2):
            pieces = [inverses[panel, :, y * 256 + z * 32 : y * 256 + z * 32 + 32] for y in range(4)]
            out[z, :, 256 + panel * 128 : 384 + panel * 128] = jnp.concatenate(pieces, axis=1)


def couple_kernel(tiles, out):
    out[...] = lax.dot_general(
        tiles[:, 0:128],
        tiles[:, 256:384],
        (((0,), (0,)), ((), ())),
        precision=EXACT,
        preferred_element_type=F32,
    )


def chain_kernel(tiles, part0, got1, got2, got3, out):
    at = got1.shape[0] - 128
    total = (part0[...] + got1[at:, :]) + (got2[at:, :] + got3[at:, :])
    out[...] = jnp.dot(tiles[:, 128:256], total, precision=EXACT, preferred_element_type=F32)


def sum_kernel(a, b, out):
    out[...] = a[...] + b[...]


def gather_sums_kernel(a, b, c, d, rider, own, *outs):
    size = own.shape[0]
    for j, out in enumerate((own,) + outs):
        span = slice(j * size, (j + 1) * size)
        out[0:size, :] = (a[span, :] + b[span, :]) + (c[span, :] + d[span, :])
        if j and out.shape[0] > size:
            out[size:, :] = rider[...]


def gather_sums(parts, rider, count, carried):
    size = parts[0].shape[0] // count
    longer = jax.ShapeDtypeStruct((size + (rider.shape[0] if carried else 0), 128), F32)
    return pl.pallas_call(
        gather_sums_kernel,
        out_shape=[jax.ShapeDtypeStruct((size, 128), F32)] + [longer] * (count - 1),
        in_specs=[pl.BlockSpec()] * len(parts) + [pl.BlockSpec() if carried else ORDER],
        compiler_params=SMALL,
    )(*parts, rider)


def interleave_kernel(a0, a1, a2, a3, b0, b1, b2, b3, out):
    size = a0.shape[0]
    low = (a0[...] + a1[0:size, :]) + (a2[0:size, :] + a3[0:size, :])
    high = (b0[...] + b1[...]) + (b2[...] + b3[...])
    nz = out.shape[0]
    for z in range(nz):
        span = slice(z * 32, (z + 1) * 32)
        out[z, 0:32, :] = low[span, :]
        out[z, 32:64, :] = high[span, :] if z < nz - 1 else low[nz * 32 :, :]


def apply_kernel(place, tiles, mix0, mix1, mix2, mix3, rest0, rest1, rest2, rest3, out, first, second):
    ny = 4
    for step, rest in enumerate((rest0, rest1, rest2, rest3)):
        at = pl.multiple_of(lax.rem(place[1] + ny - step, ny) * 32, 32)
        first[pl.ds(at, 32), :] = rest[0:32, :]
        second[pl.ds(at, 32), :] = rest[32:64, :]
    mix = (mix0[...] + mix1[...]) + (mix2[...] + mix3[...])
    low = jnp.dot(tiles[:, 256:384], first[...], precision=EXACT, preferred_element_type=F32)
    high = jnp.dot(tiles[:, 384:512], second[...], precision=EXACT, preferred_element_type=F32)
    high = high - jnp.dot(mix, first[...], precision=EXACT, preferred_element_type=F32)
    for z in range(out.shape[0]):
        out[z, 0:32, :] = low[z * 32 : (z + 1) * 32, :]
        out[z, 32:64, :] = high[z * 32 : (z + 1) * 32, :]


def steps(panel_rows, solved, right_side, coupling, inverses):
    nx, ny, nz, nc = (lax.axis_size(a) for a in ("x", "y", "z", "core"))
    x, y, core = lax.axis_index("x"), lax.axis_index("y"), lax.axis_index("core")
    own = jnp.stack([x, y, core]).astype(jnp.int32)
    other = jnp.stack([x, y, 1 - core]).astype(jnp.int32)

    to_partner0, panel_rows, solved = first_products(other, panel_rows, solved, nx, ny, nz)
    from_partner0 = shift(to_partner0, "core", 1, nc)
    to_partner1 = products(other, 1, panel_rows, solved, None, False, nx, ny, nz)
    from_partner1 = shift(to_partner1, "core", 1, nc)
    blocks0 = products(own, 0, panel_rows, solved, from_partner0, True, nx, ny, nz)
    got0 = [blocks0[0]] + [shift(blocks0[j], "x", j, nx) for j in range(1, nx)]
    blocks1 = products(own, 1, panel_rows, solved, from_partner1, False, nx, ny, nz)
    got1 = [blocks1[0]] + [shift(blocks1[j], "y", j, ny) for j in range(1, ny)]

    packed = pl.pallas_call(
        pack_kernel,
        out_shape=jax.ShapeDtypeStruct((nz, 32, 512), F32),
        in_specs=[SMEM, pl.BlockSpec(), pl.BlockSpec()],
        compiler_params=SMALL,
    )(own, inverses, coupling.T)
    tiles = lax.all_to_all(packed, "z", 0, 0, tiled=True).reshape(nz * 32, 512)

    coupled = pl.pallas_call(
        couple_kernel, out_shape=jax.ShapeDtypeStruct((128, 128), F32), compiler_params=SMALL
    )(tiles)
    sums0 = gather_sums(got0, coupled, ny, True)
    again0 = [sums0[0]] + [shift(sums0[j], "y", j, ny) for j in range(1, ny)]
    sums1 = gather_sums(got1, coupled, nx, False)
    again1 = [sums1[0]] + [shift(sums1[j], "x", j, nx) for j in range(1, nx)]
    chained = pl.pallas_call(
        chain_kernel, out_shape=jax.ShapeDtypeStruct((256, 128), F32), compiler_params=SMALL
    )(tiles, coupled, *again0[1:])
    chained_of_partner = shift(chained, "core", 1, nc)
    by_z = pl.pallas_call(
        interleave_kernel,
        out_shape=jax.ShapeDtypeStruct((nz, 64, 128), F32),
        compiler_params=SMALL,
    )(*again0, *again1)
    mix = pl.pallas_call(
        sum_kernel, out_shape=jax.ShapeDtypeStruct((256, 128), F32), compiler_params=SMALL
    )(chained, chained_of_partner)
    mixes = [mix] + [shift(mix, "x", j, nx) for j in range(1, nx)]
    old = lax.all_to_all(by_z, "z", 0, 0, tiled=True).sum(axis=0)
    rest = right_side.reshape(64, 128) - old

    rests = [rest] + [shift(rest, "y", j, ny) for j in range(1, ny)]
    solved_part = pl.pallas_call(
        apply_kernel,
        out_shape=jax.ShapeDtypeStruct((nz, 64, 128), F32),
        in_specs=[SMEM] + [pl.BlockSpec()] * 9,
        scratch_shapes=[pltpu.VMEM((128, 128), F32), pltpu.VMEM((128, 128), F32)],
        compiler_params=SMALL,
    )(own, tiles, *mixes, *rests)
    panels = lax.all_to_all(solved_part, "z", 0, 0, tiled=True).sum(axis=0)
    return panels.reshape(right_side.shape)


def solution(mesh):
    finer = Mesh(mesh.devices.reshape(4, 8, 4, 2), AXES)
    prow, pcol = ("y", "z"), ("x", "core")
    return jax.shard_map(
        steps,
        mesh=finer,
        in_specs=(
            P(None, None, AXES),
            P(AXES, None),
            P(None, prow, pcol),
            P(None, prow),
            P(None, prow, None),
        ),
        out_specs=P(None, prow, pcol),
        check_vma=False,
    )
```
